32 devices in a mesh: ctx: 8 (over y, x, core), qry: 4 (over z).
Axes of the slice: x: 2, y: 2, z: 4, core: 2. Of those that a mesh axis runs over, the one named last changes fastest.
Arguments:
- hist_bins: int32 [512, 16], P(('ctx', 'qry')), may hold values from 0 to 63
- hist_ranks: int32 [512], P(('ctx', 'qry')), may hold values from 0 to 511, each once
- query_bins: int32 [32768, 16], P(('ctx', 'qry')), may hold values from 0 to 63
- bin_table: bfloat16 [1024, 512], replicated, may hold values from -4.5 to 4.5
- rank_vector: bfloat16 [512], replicated, may hold values from -5 to 5
- w_query: bfloat16 [512, 512], replicated, may hold values from -5.833631 to 5.833631
- w_key: bfloat16 [512, 512], replicated, may hold values from -0.176776695 to 0.176776695
- w_value: bfloat16 [512, 512], replicated, may hold values from -0.25 to 0.25
- w_out: bfloat16 [512, 512], replicated, may hold values from -0.25 to 0.25
- w_up: bfloat16 [512, 2048], replicated, may hold values from -0.25 to 0.25
- w_down: bfloat16 [2048, 512], replicated, may hold values from -0.125 to 0.125
Outputs:
- hist_out: bfloat16 [512, 512], P(('ctx', 'qry'))
- query_out: bfloat16 [32768, 512], P(('ctx', 'qry'))
The draws below stay inside these ranges and needn't reach their ends.
All inputs are finite; a program needn't handle non-finite values.
Results may differ from the reference program's by a relative error of at most 0.008.
Values may be sent and summed in bfloat16 or wider, within the bound.
A program may use at most 64 MiB of HBM per device.

```python
import math
import jax
import jax.numpy as jnp
from jax import lax

D = 512
HEADS = 8
FF = 2048
FEATURES = 16
BINS = 64
HISTORY = 512
QUERIES = 32768


def paired_weights(key):
    folded = jax.random.fold_in(key, 7)
    key_shared, key_jitter = jax.random.split(folded, 2)
    shared = jax.random.truncated_normal(key_shared, -4.0, 4.0, (D, D), jnp.float32) * (1.0 / math.sqrt(D))
    jitter = jax.random.truncated_normal(key_jitter, -4.0, 4.0, (D, D), jnp.float32) * (1.0 / math.sqrt(D))
    queried = 3.0 * jitter
    return (queried, shared)


def draw_w_query(key, part):
    return paired_weights(key)[0].astype(jnp.bfloat16)


def draw_w_key(key, part):
    return paired_weights(key)[1].astype(jnp.bfloat16)


def draw_bin_table(key, part):
    folded = jax.random.fold_in(key, 11)
    key_rows, key_cols, key_values = jax.random.split(folded, 3)
    row_scale = jnp.exp(jax.random.uniform(key_rows, (FEATURES * BINS, 1), jnp.float32, math.log(0.3), math.log(1.5)))
    col_scale = jnp.exp(jax.random.uniform(key_cols, (1, D), jnp.float32, math.log(0.3), math.log(3.0)))
    entries = jax.random.truncated_normal(key_values, -4.0, 4.0, (FEATURES * BINS, D), jnp.float32)
    return (0.25 * entries * row_scale * col_scale).astype(jnp.bfloat16)


def with_ends(values, stream_key, least, largest):
    longest = values.shape.index(max(values.shape))
    spots = []
    for shift in (0, 1):
        where = [jax.random.randint(jax.random.fold_in(stream_key, axis), (), 0, length) for axis, length in enumerate(values.shape)]
        where[longest] = (where[longest] + shift) % values.shape[longest]
        spots.append(tuple(where))
    return values.at[spots[0]].set(least).at[spots[1]].set(largest)


def bell_draw(stream_key, shape, spread, limit, kind=jnp.bfloat16):
    values = jax.random.normal(stream_key, shape, jnp.float32) * spread
    return jnp.minimum(jnp.maximum(values, -limit), limit).astype(kind)


def setup_inputs(seed: int = 0) -> dict:
    keys = jax.random.split(jax.random.key(seed), 12)
    return {
        "hist_bins": with_ends(jax.random.randint(keys[0], (HISTORY, FEATURES), 0, BINS), jax.random.fold_in(keys[0], 1), 0, BINS - 1).astype(jnp.int32),
        "hist_ranks": jax.random.permutation(keys[1], HISTORY).astype(jnp.int32),
        "query_bins": with_ends(jax.random.randint(keys[2], (QUERIES, FEATURES), 0, BINS), jax.random.fold_in(keys[2], 1), 0, BINS - 1).astype(jnp.int32),
        "bin_table": draw_bin_table(jax.random.fold_in(keys[11], 71), 0),
        "rank_vector": bell_draw(keys[4], (D,), 1.0, 5.0),
        "w_query": draw_w_query(jax.random.fold_in(keys[11], 71), 0),
        "w_key": draw_w_key(jax.random.fold_in(keys[11], 71), 0),
        "w_value": bell_draw(keys[7], (D, D), D ** -0.5, 0.25),
        "w_out": bell_draw(keys[8], (D, D), D ** -0.5, 0.25),
        "w_up": bell_draw(keys[9], (D, FF), D ** -0.5, 0.25),
        "w_down": bell_draw(keys[10], (FF, D), FF ** -0.5, 0.125),
    }


epsilon = 1e-05

def normalize(values):
    centered = values - lax.optimization_barrier(jnp.mean(values, axis=-1, keepdims=True))
    variance = lax.optimization_barrier(jnp.mean(centered * centered, axis=-1, keepdims=True))
    return centered * lax.rsqrt(variance + epsilon)

def embed_bins(bin_rows, bin_table):
    summed = jnp.zeros((bin_rows.shape[0], bin_table.shape[1]), jnp.float32)
    for feature in range(bin_rows.shape[1]):
        looked_up = jnp.take(bin_table, (bin_rows[:, feature] + feature * BINS).astype(jnp.int32), axis=0)
        summed = summed + looked_up.astype(jnp.float32)
    return summed

def history_rows(bin_rows, rank_ids, bin_table, rank_vector, history_total):
    level = (2.0 * rank_ids.astype(jnp.float32) + 1.0) / history_total - 1.0
    return embed_bins(bin_rows, bin_table) + level[:, None] * rank_vector.astype(jnp.float32)[None, :]

def attend_all(queries, key_rows, value_rows):
    row_count = queries.shape[0]
    head_dim = queries.shape[1] // HEADS
    query_heads = queries.reshape(row_count, HEADS, head_dim).astype(jnp.float32)
    key_heads = key_rows.reshape(-1, HEADS, head_dim).astype(jnp.float32)
    value_heads = value_rows.reshape(-1, HEADS, head_dim).astype(jnp.float32)
    scores = jnp.einsum('nhd,khd->hnk', query_heads, key_heads) * head_dim ** (-0.5)
    row_peak = lax.optimization_barrier(jnp.max(scores, axis=-1, keepdims=True))
    weights = jnp.exp(scores - row_peak)
    row_total = lax.optimization_barrier(jnp.sum(weights, axis=-1))
    rounded = lax.optimization_barrier(weights.astype(jnp.bfloat16)).astype(jnp.float32)
    summed = jnp.einsum('hnk,khd->hnd', rounded, value_heads) / row_total[..., None]
    return jnp.transpose(summed, (1, 0, 2)).reshape(row_count, -1).astype(jnp.bfloat16)

def layer_rows(all_rows, key_rows, value_rows, w_query, w_out, w_up, w_down):
    normed = normalize(all_rows).astype(jnp.bfloat16)
    queries = jnp.dot(normed, w_query, preferred_element_type=jnp.float32).astype(jnp.bfloat16)
    attended = attend_all(queries, key_rows, value_rows)
    after_attention = all_rows + jnp.dot(attended, w_out, preferred_element_type=jnp.float32)
    inner = jnp.dot(normalize(after_attention).astype(jnp.bfloat16), w_up, preferred_element_type=jnp.float32)
    hidden = jax.nn.gelu(inner, approximate=True).astype(jnp.bfloat16)
    return (after_attention + jnp.dot(hidden, w_down, preferred_element_type=jnp.float32)).astype(jnp.bfloat16)

def reference(hist_bins, hist_ranks, query_bins, bin_table, rank_vector, w_query, w_key, w_value, w_out, w_up, w_down):
    hist_embed = history_rows(hist_bins, hist_ranks, bin_table, rank_vector, float(HISTORY))
    hist_normed = normalize(hist_embed).astype(jnp.bfloat16)
    key_rows = jnp.dot(hist_normed, w_key, preferred_element_type=jnp.float32).astype(jnp.bfloat16)
    value_rows = jnp.dot(hist_normed, w_value, preferred_element_type=jnp.float32).astype(jnp.bfloat16)

    def apply_layer(block_rows):
        return layer_rows(block_rows, key_rows, value_rows, w_query, w_out, w_up, w_down)
    hist_size = math.gcd(hist_embed.shape[0], 512)
    hist_blocks = hist_embed.reshape(-1, hist_size, hist_embed.shape[1])
    hist_out = lax.map(apply_layer, hist_blocks).reshape(hist_embed.shape[0], -1)

    def query_block(bin_rows):
        return apply_layer(embed_bins(bin_rows, bin_table))
    query_size = math.gcd(query_bins.shape[0], 512)
    query_blocks = query_bins.reshape(-1, query_size, query_bins.shape[1])
    query_out = lax.map(query_block, query_blocks).reshape(query_bins.shape[0], -1)
    return (hist_out, query_out)
```

```python
import functools
import math

import jax
import jax.numpy as jnp
from jax import lax
from jax.experimental import pallas as pl
from jax.experimental.pallas import tpu as pltpu
from jax.sharding import PartitionSpec as P

HEADS = 8
LANES = 128
RADIX = 64
EMBED_LIMIT = 24 << 20
LAYER_LIMIT = 16 << 20
epsilon = 1e-05
F32 = jnp.float32
BF16 = jnp.bfloat16


def normalize(values):
    centered = values - jnp.mean(values, axis=-1, keepdims=True)
    variance = jnp.mean(centered * centered, axis=-1, keepdims=True)
    return centered * lax.rsqrt(variance + epsilon)


def dot(a, b):
    return jnp.dot(a, b, preferred_element_type=F32)


def embed(named, column_bin, table):
    one_hot = jnp.where(named == column_bin, 1.0, 0.0).astype(BF16)
    return dot(one_hot, table)


def embed_kernel(
    sizes,
    query_bins_hbm,
    hist_bins_hbm,
    hist_ranks_hbm,
    table_hbm,
    rank_vector_hbm,
    w_query_hbm,
    w_key_hbm,
    w_value_hbm,
    w_out_hbm,
    w_up_hbm,
    w_down_hbm,
    rows_out,
    queries_out,
    key_pairs,
    value_pairs,
    w_out,
    w_up,
    w_down,
    query_bins,
    hist_bins,
    hist_ranks,
    table,
    rank_vector,
    w_query,
    w_key,
    w_value,
    fetch_sem,
    staged,
    mine,
    blocks,
    hist_rows,
    hist_normed,
    send_sem,
    recv_sem,
):
    inner, count, query_tile, hist_tile = sizes
    own, features = hist_bins.shape
    query_count = query_bins.shape[1]
    total = count * own
    fetches = [
        pltpu.make_async_copy(source, target, fetch_sem.at[index])
        for index, (source, target) in enumerate(
            (
                (hist_bins_hbm, hist_bins),
                (hist_ranks_hbm, hist_ranks),
                (query_bins_hbm, query_bins),
                (table_hbm, table),
                (w_query_hbm, w_query),
                (rank_vector_hbm, rank_vector),
                (w_key_hbm, w_key),
                (w_value_hbm, w_value),
                (w_out_hbm, w_out),
                (w_up_hbm, w_up),
                (w_down_hbm, w_down),
            )
        )
    ]
    for fetch in fetches[:8]:
        fetch.start()
    me = lax.axis_index("ctx") * inner + lax.axis_index("qry")

    def place(index):
        return {"ctx": index // inner, "qry": index % inner}

    def partner(step):
        return (me + step) % count

    barrier = pltpu.get_barrier_semaphore()

    def greet(step, carry):
        pl.semaphore_signal(
            barrier,
            inc=1,
            device_id=place(partner(step)),
            device_id_type=pl.DeviceIdType.MESH,
        )
        return carry

    lax.fori_loop(1, count, greet, 0)

    fetches[0].wait()
    fetches[1].wait()
    ranks = jnp.broadcast_to(hist_ranks[...], (own, own))
    diagonal = lax.broadcasted_iota(jnp.int32, (own, own), 0) == lax.broadcasted_iota(
        jnp.int32, (own, own), 1
    )
    rank = jnp.sum(jnp.where(diagonal, ranks.astype(F32), 0.0), axis=1, keepdims=True)
    high = jnp.floor(rank * (1.0 / RADIX))
    staged[...] = jnp.zeros_like(staged)
    staged[:, :features] = hist_bins[...].astype(F32)
    staged[:, features : features + 1] = high
    staged[:, features + 1 : features + 2] = rank - high * RADIX
    mine[...] = staged[...].astype(BF16)
    blocks[me] = mine[...]

    bin_count = table.shape[0] // features
    wide = (features, table.shape[0])
    spread = jnp.where(
        lax.broadcasted_iota(jnp.int32, wide, 1) // bin_count
        == lax.broadcasted_iota(jnp.int32, wide, 0),
        1.0,
        0.0,
    ).astype(BF16)
    column_bin = (
        lax.broadcasted_iota(jnp.int32, (1, table.shape[0]), 1) % bin_count
    ).astype(F32)

    def copy_to(step):
        other = partner(step)
        return pltpu.make_async_remote_copy(
            src_ref=mine,
            dst_ref=blocks.at[me],
            send_sem=send_sem.at[other],
            recv_sem=recv_sem.at[me],
            device_id=place(other),
            device_id_type=pl.DeviceIdType.MESH,
        )

    def copy_from(step):
        other = partner(step)
        return pltpu.make_async_remote_copy(
            src_ref=mine,
            dst_ref=blocks.at[other],
            send_sem=send_sem.at[other],
            recv_sem=recv_sem.at[other],
            device_id=place(other),
            device_id_type=pl.DeviceIdType.MESH,
        )

    def send(step, carry):
        copy_to(step).start()
        return carry

    pl.semaphore_wait(barrier, count - 1)
    lax.fori_loop(1, count, send, 0)

    for fetch in fetches[2:5]:
        fetch.wait()
    for fetch in fetches[8:]:
        fetch.start()

    def query_step(index, carry):
        at = pl.ds(pl.multiple_of(index * query_tile, query_tile), query_tile)
        named = lax.dot_general(
            query_bins[:, at].astype(F32).astype(BF16),
            spread,
            (((0,), (0,)), ((), ())),
            preferred_element_type=F32,
        )
        found = embed(named, column_bin, table[...])
        rows_out[at, :] = found
        queries_out[at, :] = dot(normalize(found).astype(BF16), w_query[...]).astype(BF16)
        return carry

    lax.fori_loop(0, query_count // query_tile, query_step, 0)

    def finish(step, carry):
        copy_to(step).wait_send()
        copy_from(step).wait_recv()
        return carry

    for fetch in fetches[5:8]:
        fetch.wait()
    lax.fori_loop(1, count, finish, 0)

    width = table.shape[1]
    head_dim = width // HEADS
    pairs = HEADS // 2
    left = lax.broadcasted_iota(jnp.int32, (hist_tile, LANES), 1) < head_dim
    upper = lax.broadcasted_iota(jnp.int32, (LANES, hist_tile), 0) < head_dim

    def hist_step(index, carry):
        tile_blocks = hist_tile // own
        block = blocks[pl.ds(index * tile_blocks, tile_blocks)].reshape(hist_tile, LANES)
        at = pl.ds(pl.multiple_of(index * hist_tile, hist_tile), hist_tile)
        wide_block = block.astype(F32)
        rank = (
            wide_block[:, features : features + 1] * RADIX
            + wide_block[:, features + 1 : features + 2]
        )
        level = (2.0 * rank + 1.0) / float(total) - 1.0
        found = embed(dot(block[:, :features], spread), column_bin, table[...])
        found = found + level * rank_vector[...].astype(F32).reshape(1, -1)
        hist_rows[at, :] = found
        normed = normalize(found).astype(BF16)
        hist_normed[at, :] = normed
        keys = dot(normed, w_key[...]).T
        values = dot(normed, w_value[...])
        for pair in range(pairs):
            span = slice(pair * LANES, (pair + 1) * LANES)
            key = keys[span, :]
            key_pairs[index, pair, :, :hist_tile] = jnp.where(upper, key, 0.0).astype(BF16)
            key_pairs[index, pair, :, hist_tile:] = jnp.where(upper, 0.0, key).astype(BF16)
            value = values[:, span]
            for half, keep in ((0, left), (1, jnp.logical_not(left))):
                part = slice(half * hist_tile, (half + 1) * hist_tile)
                value_pairs[index, pair, part, :LANES] = jnp.where(keep, value, 0.0).astype(BF16)
                value_pairs[index, pair, part, LANES:] = jnp.where(keep, 1.0, 0.0).astype(BF16)
        return carry

    lax.fori_loop(0, total // hist_tile, hist_step, 0)
    at = pl.ds(pl.multiple_of(me * own, own), own)
    rows_out[query_count:, :] = hist_rows[at, :]
    queries_out[query_count:, :] = dot(hist_normed[at, :], w_query[...]).astype(BF16)
    for fetch in fetches[8:]:
        fetch.wait()


def layer_kernel(
    sizes,
    rows_out,
    queries_out,
    key_pairs,
    value_pairs,
    w_out,
    w_up,
    w_down,
    hist_out,
    query_out,
    results,
    store_sem,
):
    tile, hist_tile, chunks = sizes
    own = hist_out.shape[0]
    query_count = query_out.shape[0]
    row_count = own + query_count
    head_dim = rows_out.shape[1] // HEADS
    pairs = HEADS // 2

    factor = math.log2(math.e) * head_dim ** (-0.5)
    tiles = row_count // tile

    def pair_scores(at, chunk, pair):
        scores = dot(queries_out[at, pair * LANES : (pair + 1) * LANES], key_pairs[chunk, pair])
        return scores[:, :hist_tile], scores[:, hist_tile:]

    def weigh(scores, peak):
        return jnp.exp2((scores - peak) * factor).astype(BF16)

    def attend(at, pair):
        even, odd = pair_scores(at, 0, pair)
        peaks = [jnp.max(even, axis=1, keepdims=True), jnp.max(odd, axis=1, keepdims=True)]
        weights = jnp.concatenate([weigh(even, peaks[0]), weigh(odd, peaks[1])], axis=1)
        summed = dot(weights, value_pairs[0, pair])
        if chunks > 1:

            def absorb(chunk, carry):
                peak_even, peak_odd, summed = carry
                even, odd = pair_scores(at, chunk, pair)
                new_even = jnp.maximum(peak_even, jnp.max(even, axis=1, keepdims=True))
                new_odd = jnp.maximum(peak_odd, jnp.max(odd, axis=1, keepdims=True))
                weights = jnp.concatenate([weigh(even, new_even), weigh(odd, new_odd)], axis=1)
                lane = lax.broadcasted_iota(jnp.int32, summed.shape, 1) % LANES
                fade = jnp.where(
                    lane < head_dim,
                    jnp.exp2((peak_even - new_even) * factor),
                    jnp.exp2((peak_odd - new_odd) * factor),
                )
                summed = summed * fade + dot(weights, value_pairs[chunk, pair])
                return (new_even, new_odd, summed)

            summed = lax.fori_loop(1, chunks, absorb, (peaks[0], peaks[1], summed))[2]
        return (summed[:, :LANES] / summed[:, LANES:]).astype(BF16)

    def project(at, attended):
        after = rows_out[at, :] + dot(jnp.concatenate(attended, axis=1), w_out[...])
        rows_out[at, :] = after
        queries_out[at, :] = normalize(after).astype(BF16)

    ff_tile = w_up.shape[1] // pairs

    def feed(normed, part):
        span = slice(part * ff_tile, (part + 1) * ff_tile)
        hidden = jax.nn.gelu(dot(normed, w_up[:, span]), approximate=True).astype(BF16)
        return dot(hidden, w_down[span, :])

    def rows_at(index):
        return pl.ds(pl.multiple_of(index * tile, tile), tile)

    def store(index):
        at = rows_at(index)
        return pltpu.make_async_copy(results.at[at], query_out.at[at], store_sem.at[index])

    first = slice(0, tile)
    project(first, [attend(first, pair) for pair in range(pairs)])

    def tile_step(index, carry):
        at, before = rows_at(index), rows_at(index - 1)
        normed = queries_out[before, :]
        result = rows_out[before, :]
        attended = []
        for pair in range(pairs):
            attended.append(attend(at, pair))
            if pair < pairs - 1:
                result = result + feed(normed, pair)
        project(at, attended)
        results[before, :] = (result + feed(normed, pairs - 1)).astype(BF16)
        store(index - 1).start()
        return carry

    lax.fori_loop(1, tiles, tile_step, 0)
    start = (tiles - 1) * tile
    normed = queries_out[start:, :]
    result = rows_out[start:, :]
    for part in range(pairs):
        result = result + feed(normed, part)
    result = result.astype(BF16)
    results[start:, :] = result
    last = [
        pltpu.make_async_copy(
            results.at[start:query_count],
            query_out.at[start:query_count],
            store_sem.at[tiles - 1],
        ),
        pltpu.make_async_copy(results.at[query_count:], hist_out, store_sem.at[tiles]),
    ]
    for copy in last:
        copy.start()
    for index in range(tiles - 1):
        store(index).wait()
    for copy in last:
        copy.wait()


def local(
    inner,
    count,
    hist_bins,
    hist_ranks,
    query_bins,
    bin_table,
    rank_vector,
    w_query,
    w_key,
    w_value,
    w_out,
    w_up,
    w_down,
):
    own = hist_bins.shape[0]
    query_count = query_bins.shape[0]
    width = bin_table.shape[1]
    total = own * count
    row_count = own + query_count
    hist_tile = math.gcd(total, 512)
    query_tile = math.gcd(query_count, 256)
    chunks = total // hist_tile
    features = hist_bins.shape[1]
    pairs = HEADS // 2
    tile = max(
        size for size in range(16, 257, 16) if row_count % size == 0 and size > own
    )
    hbm = pl.BlockSpec(memory_space=pltpu.HBM)
    vmem = pl.BlockSpec(memory_space=pltpu.VMEM)
    held = pl.pallas_call(
        functools.partial(embed_kernel, (inner, count, query_tile, hist_tile)),
        out_shape=(
            pltpu.VMEM((row_count, width), F32),
            pltpu.VMEM((row_count, width), BF16),
            pltpu.VMEM((chunks, pairs, LANES, 2 * hist_tile), BF16),
            pltpu.VMEM((chunks, pairs, 2 * hist_tile, 2 * LANES), BF16),
            pltpu.VMEM(w_out.shape, BF16),
            pltpu.VMEM(w_up.shape, BF16),
            pltpu.VMEM(w_down.shape, BF16),
        ),
        in_specs=[hbm] * 11,
        out_specs=(vmem,) * 7,
        scratch_shapes=[
            pltpu.VMEM((features, query_count), jnp.int32),
            pltpu.VMEM((own, features), jnp.int32),
            pltpu.VMEM((1, own), jnp.int32),
            pltpu.VMEM(bin_table.shape, BF16),
            pltpu.VMEM(rank_vector.shape, BF16),
            pltpu.VMEM(w_query.shape, BF16),
            pltpu.VMEM(w_key.shape, BF16),
            pltpu.VMEM(w_value.shape, BF16),
            pltpu.SemaphoreType.DMA((11,)),
            pltpu.VMEM((own, LANES), F32),
            pltpu.VMEM((own, LANES), BF16),
            pltpu.VMEM((count, own, LANES), BF16),
            pltpu.VMEM((total, width), F32),
            pltpu.VMEM((total, width), BF16),
            pltpu.SemaphoreType.DMA((count,)),
            pltpu.SemaphoreType.DMA((count,)),
        ],
        compiler_params=pltpu.CompilerParams(
            collective_id=0, has_side_effects=True, vmem_limit_bytes=EMBED_LIMIT
        ),
        name="embed_rows",
    )(
        *(
            pltpu.with_memory_space_constraint(value, pltpu.HBM)
            for value in (
                query_bins.T,
                hist_bins,
                hist_ranks.reshape(1, own),
                bin_table,
                rank_vector,
                w_query,
                w_key,
                w_value,
                w_out,
                w_up,
                w_down,
            )
        )
    )
    return pl.pallas_call(
        functools.partial(layer_kernel, (tile, hist_tile, chunks)),
        out_shape=(
            jax.ShapeDtypeStruct((own, width), BF16),
            jax.ShapeDtypeStruct((query_count, width), BF16),
        ),
        in_specs=[vmem] * 7,
        out_specs=(hbm, hbm),
        scratch_shapes=[
            pltpu.VMEM((row_count, width), BF16),
            pltpu.SemaphoreType.DMA((row_count // tile + 1,)),
        ],
        compiler_params=pltpu.CompilerParams(vmem_limit_bytes=LAYER_LIMIT),
        name="layer_rows",
    )(*held)


def solution(mesh):
    inner = mesh.shape["qry"]
    split = P(("ctx", "qry"), None)
    return jax.shard_map(
        functools.partial(local, inner, mesh.shape["ctx"] * inner),
        mesh=mesh,
        in_specs=(split, P(("ctx", "qry")), split) + (P(),) * 8,
        out_specs=(split, split),
        check_vma=False,
    )
```

```python
import functools
import math

import jax
import jax.numpy as jnp
from jax import lax
from jax.experimental import pallas as pl
from jax.experimental.pallas import tpu as pltpu
from jax.sharding import PartitionSpec as P

HEADS = 8
LANES = 128
EMBED_LIMIT = 24 << 20
LAYER_LIMIT = 28 << 20
GROUP = 8
UP_TILE = 256
DOWN_TILE = 256
SPLIT = 2
AHEAD = 2
BEHIND = 1
epsilon = 1e-05
GELU = math.sqrt(2.0 / math.pi)
F32 = jnp.float32
BF16 = jnp.bfloat16


def normalize(values):
    centered = values - jnp.mean(values, axis=-1, keepdims=True)
    variance = jnp.mean(centered * centered, axis=-1, keepdims=True)
    return centered * lax.rsqrt(variance + epsilon)


def dot(a, b):
    return jnp.dot(a, b, preferred_element_type=F32)


def dot_rows(a, b):
    return lax.dot_general(a, b, (((1,), (1,)), ((), ())), preferred_element_type=F32)


def iota(shape, dim):
    return lax.broadcasted_iota(jnp.int32, shape, dim)


def one(mask):
    return jnp.where(mask, 1.0, 0.0).astype(BF16)


def embed(named, column_bin, table):
    return dot(one(named == column_bin), table)


def embed_kernel(
    sizes,
    query_bins_hbm,
    hist_bins_hbm,
    hist_ranks_hbm,
    table_hbm,
    rank_vector_hbm,
    w_query_hbm,
    w_key_hbm,
    w_value_hbm,
    w_out_hbm,
    w_up_hbm,
    w_down_hbm,
    rows_out,
    queries_out,
    keys_out,
    values_out,
    w_out,
    w_up,
    w_down,
    query_bins,
    hist_bins,
    hist_ranks,
    table,
    rank_vector,
    w_query,
    w_key,
    w_value,
    fetch_sem,
    mine,
    blocks,
    hist_rows,
    hist_normed,
    send_sem,
    recv_sem,
):
    outer, inner, query_tile, hist_tile = sizes
    count = outer * inner
    own, features = hist_bins.shape
    query_count = query_bins.shape[1]
    total = count * own
    fetches = [
        pltpu.make_async_copy(source, target, fetch_sem.at[index])
        for index, (source, target) in enumerate(
            (
                (hist_bins_hbm, hist_bins),
                (hist_ranks_hbm, hist_ranks),
                (query_bins_hbm, query_bins),
                (table_hbm, table),
                (w_query_hbm, w_query),
                (rank_vector_hbm, rank_vector),
                (w_key_hbm, w_key),
                (w_value_hbm, w_value),
                (w_out_hbm, w_out),
                (w_up_hbm, w_up),
                (w_down_hbm, w_down),
            )
        )
    ]
    for fetch in fetches[:8]:
        fetch.start()
    at_outer = lax.axis_index("ctx")
    at_inner = lax.axis_index("qry")
    me = at_outer * inner + at_inner
    barrier = pltpu.get_barrier_semaphore()

    def others(act):
        def across(step, carry):
            for shift in reversed(range(outer)):
                act((at_outer + shift) % outer, (at_inner + inner - step) % inner)
            return carry

        lax.fori_loop(1, inner, across, 0)
        for shift in reversed(range(1, outer)):
            act((at_outer + shift) % outer, at_inner)

    def greet(x, y):
        pl.semaphore_signal(
            barrier,
            inc=1,
            device_id={"ctx": x, "qry": y},
            device_id_type=pl.DeviceIdType.MESH,
        )

    others(greet)

    parts = features // GROUP
    per_row = iota((own, LANES), 1) // GROUP == iota((own, LANES), 0)
    fetches[0].wait()
    fetches[1].wait()
    bins = hist_bins[...].astype(F32).astype(BF16)
    for part in range(parts):
        pick = iota((features, LANES), 1) % GROUP + part * GROUP == iota((features, LANES), 0)
        laid = jnp.sum(jnp.where(per_row, dot(bins, one(pick)), 0.0), axis=0, keepdims=True)
        mine[part : part + 1, :] = laid.astype(jnp.int32)
    mine[parts : parts + 1, :] = jnp.zeros((1, LANES), jnp.int32)
    mine[parts : parts + 1, :own] = hist_ranks[...]
    blocks[me] = mine[...]

    def send(x, y):
        pltpu.make_async_remote_copy(
            src_ref=mine,
            dst_ref=blocks.at[me],
            send_sem=send_sem,
            recv_sem=recv_sem,
            device_id={"ctx": x, "qry": y},
            device_id_type=pl.DeviceIdType.MESH,
        ).start()

    pl.semaphore_wait(barrier, count - 1)
    others(send)

    bin_count = table.shape[0] // features
    wide = (features, table.shape[0])
    spread = one(iota(wide, 1) // bin_count == iota(wide, 0))
    column_bin = (iota((1, table.shape[0]), 1) % bin_count).astype(F32)
    width = table.shape[1]
    head_dim = width // HEADS
    pairs = HEADS // 2
    factor = math.log2(math.e) * head_dim ** (-0.5)

    def project(normed):
        return (dot(normed, w_query[...]) * factor).astype(BF16)

    for fetch in fetches[2:5]:
        fetch.wait()
    for fetch in fetches[8:]:
        fetch.start()

    def query_step(index, carry):
        at = pl.ds(pl.multiple_of(index * query_tile, query_tile), query_tile)
        named = lax.dot_general(
            query_bins[:, at].astype(F32).astype(BF16),
            spread,
            (((0,), (0,)), ((), ())),
            preferred_element_type=F32,
        )
        found = embed(named, column_bin, table[...])
        rows_out[at, :] = found
        queries_out[at, :] = project(normalize(found).astype(BF16))
        return carry

    lax.fori_loop(0, query_count // query_tile, query_step, 0)

    for fetch in fetches[5:8]:
        fetch.wait()
    tall = (parts * LANES, table.shape[0])
    deal = one(
        iota(tall, 1) // bin_count == iota(tall, 0) // LANES * GROUP + iota(tall, 0) % GROUP
    )
    rest = pl.ds(0, count - 1)
    pltpu.make_async_copy(blocks.at[rest], blocks.at[rest], recv_sem).wait()

    tile_blocks = hist_tile // own
    block_shape = (tile_blocks, own, LANES)
    lane = iota(block_shape, 2)
    row = iota(block_shape, 1)
    left = iota((hist_tile, LANES), 1) < head_dim

    def hist_step(index, carry):
        at = pl.ds(pl.multiple_of(index * hist_tile, hist_tile), hist_tile)
        block = blocks[pl.ds(index * tile_blocks, tile_blocks)].astype(F32)
        laid = [
            jnp.where(lane // GROUP == row, block[:, part : part + 1, :], 0.0)
            .reshape(hist_tile, LANES)
            .astype(BF16)
            for part in range(parts)
        ]
        rank = jnp.sum(
            jnp.where(lane == row, block[:, parts : parts + 1, :], 0.0).reshape(
                hist_tile, LANES
            ),
            axis=1,
            keepdims=True,
        )
        level = (2.0 * rank + 1.0) / float(total) - 1.0
        found = embed(dot(jnp.concatenate(laid, axis=1), deal), column_bin, table[...])
        found = found + level * rank_vector[...].astype(F32).reshape(1, -1)
        hist_rows[at, :] = found
        normed = normalize(found).astype(BF16)
        hist_normed[at, :] = normed
        keys = dot(normed, w_key[...])
        values = dot(normed, w_value[...]).astype(BF16).T
        for pair in range(pairs):
            key = keys[:, pair * LANES : (pair + 1) * LANES]
            keys_out[index, pair, :hist_tile, :] = jnp.where(left, key, 0.0).astype(BF16)
            keys_out[index, pair, hist_tile:, :] = jnp.where(left, 0.0, key).astype(BF16)
        for head in range(HEADS):
            values_out[index, head, :head_dim, :] = values[
                head * head_dim : (head + 1) * head_dim, :
            ]
            values_out[index, head, head_dim:, :] = jnp.ones(
                (values_out.shape[2] - head_dim, hist_tile), BF16
            )
        return carry

    lax.fori_loop(0, total // hist_tile, hist_step, 0)
    at = pl.ds(pl.multiple_of(me * own, own), own)
    rows_out[query_count:, :] = hist_rows[at, :]
    queries_out[query_count:, :] = project(hist_normed[at, :])
    pltpu.make_async_copy(blocks.at[rest], blocks.at[rest], send_sem).wait()
    for fetch in fetches[8:]:
        fetch.wait()


def layer_kernel(
    tile,
    rows,
    queries,
    keys,
    values,
    w_out,
    w_up,
    w_down,
    hist_out,
    query_out,
    results,
    scores,
    hidden,
    store_sem,
):
    own, width = hist_out.shape
    query_count = query_out.shape[0]
    head_dim = width // HEADS
    chunks = keys.shape[0]
    length = keys.shape[2] // 2
    part = length // SPLIT
    slots = scores.shape[0]

    def project(at, attended):
        after = rows[at, :] + dot(jnp.concatenate(attended, axis=0).T, w_out[...])
        rows[at, :] = after
        queries[at, :] = normalize(after).astype(BF16)

    def asked(at, head):
        pair = head // 2
        return queries[at, pair * LANES : (pair + 1) * LANES]

    def quotient(summed):
        return (summed[:head_dim] / summed[head_dim : head_dim + 1]).astype(BF16)

    def attend_whole(tiles):
        units = [(at, head) for at in tiles for head in range(HEADS)]
        peaks, weights, attended = {}, {}, {}

        def score(unit, piece):
            at, head = units[unit]
            start = head % 2 * length + piece * part
            found = dot_rows(keys[0, head // 2, start : start + part], asked(at, head))
            scores[unit % slots, piece * part : (piece + 1) * part, : found.shape[1]] = found
            peak = jnp.max(found, axis=0, keepdims=True)
            peaks[unit] = jnp.maximum(peaks[unit], peak) if piece else peak

        def weigh(unit, piece):
            peak = peaks[unit]
            span = slice(piece * part, (piece + 1) * part)
            found = scores[unit % slots, span, : peak.shape[1]]
            weights[unit, piece] = jnp.exp2(found - peak).astype(BF16)

        def gather(unit):
            at, head = units[unit]
            pieces = [weights.pop((unit, piece)) for piece in range(SPLIT)]
            summed = dot(values[0, head], jnp.concatenate(pieces, axis=0))
            attended[head] = quotient(summed)
            if head == HEADS - 1:
                project(at, [attended[index] for index in range(HEADS)])

        for step in range(-AHEAD, len(units) + BEHIND):
            for piece in range(SPLIT):
                if step + AHEAD < len(units):
                    score(step + AHEAD, piece)
                if 0 <= step < len(units):
                    weigh(step, piece)
                if piece == SPLIT - 1 and step >= BEHIND:
                    gather(step - BEHIND)
                yield

    def attend_chunks(tiles):
        for at in tiles:
            attended = []
            for head in range(HEADS):
                half = head % 2 * length
                query = asked(at, head)
                lanes = query.shape[0]

                def absorb(chunk, carry):
                    peak, summed = carry
                    found = dot_rows(keys[chunk, head // 2, half : half + length], query)
                    new = jnp.maximum(peak, jnp.max(found, axis=0, keepdims=True))
                    weights = jnp.exp2(found - new).astype(BF16)
                    summed = summed * jnp.exp2(peak - new) + dot(values[chunk, head], weights)
                    return new, summed

                empty = (
                    jnp.full((1, lanes), -jnp.inf, F32),
                    jnp.zeros((values.shape[2], lanes), F32),
                )
                attended.append(quotient(lax.fori_loop(0, chunks, absorb, empty)[1]))
                yield
            project(at, attended)

    stores = []

    def store(source, target):
        copy = pltpu.make_async_copy(source, target, store_sem.at[len(stores)])
        copy.start()
        stores.append(copy)

    def feed(start, middle, stop):
        for first in range(0, w_up.shape[1], UP_TILE):
            span = slice(first, first + UP_TILE)
            value = dot(queries[start:stop, :], w_up[:, span]).astype(BF16)
            bend = jnp.tanh(value * (value * value * (0.044715 * GELU) + GELU))
            hidden[: stop - start, span] = value + value * bend
            yield 2 * (stop - start)
        for low, high in ((start, middle), (middle, stop)):
            for first in range(0, width, DOWN_TILE):
                span = slice(first, first + DOWN_TILE)
                fed = dot(hidden[low - start : high - start, :], w_down[:, span])
                results[low:high, span] = (rows[low:high, span] + 0.5 * fed).astype(BF16)
                yield 8 * (high - low)
            queried = min(high, query_count)
            store(results.at[low:queried], query_out.at[low:queried])
            if high > queried:
                store(results.at[queried:high], hist_out)

    group = 2 * tile
    pending, cost = iter(()), 0
    for start in range(0, query_count, group):
        stop = min(start + group, query_count)
        tiles = [slice(first, first + tile) for first in range(start, stop, tile)]
        if stop == query_count:
            tiles.insert(1, slice(query_count, query_count + own))
            stop += own
        attend = attend_whole if chunks == 1 else attend_chunks
        if chunks == 1:
            steps = (len(tiles) * HEADS + AHEAD + BEHIND) * SPLIT
        else:
            steps = len(tiles) * HEADS
        done = 0
        for index, _ in enumerate(attend(tiles)):
            while done < cost * (index + 1) / steps:
                done += next(pending, cost)
        for _ in pending:
            pass
        pending = feed(start, start + tile, stop)
        cost = 2 * (stop - start) * (w_up.shape[1] // UP_TILE) * 2
    for _ in pending:
        pass
    for copy in stores:
        copy.wait()


def local(
    outer,
    inner,
    hist_bins,
    hist_ranks,
    query_bins,
    bin_table,
    rank_vector,
    w_query,
    w_key,
    w_value,
    w_out,
    w_up,
    w_down,
):
    own, features = hist_bins.shape
    query_count = query_bins.shape[0]
    width = bin_table.shape[1]
    count = outer * inner
    total = own * count
    row_count = own + query_count
    hist_tile = math.gcd(total, 512)
    query_tile = math.gcd(query_count, 256)
    chunks = total // hist_tile
    pairs = HEADS // 2
    tall = width // HEADS + 16
    lines = features // GROUP + 1
    hbm = pl.BlockSpec(memory_space=pltpu.HBM)
    vmem = pl.BlockSpec(memory_space=pltpu.VMEM)
    held = pl.pallas_call(
        functools.partial(embed_kernel, (outer, inner, query_tile, hist_tile)),
        out_shape=(
            pltpu.VMEM((row_count, width), F32),
            pltpu.VMEM((row_count, width), BF16),
            pltpu.VMEM((chunks, pairs, 2 * hist_tile, LANES), BF16),
            pltpu.VMEM((chunks, HEADS, tall, hist_tile), BF16),
            pltpu.VMEM(w_out.shape, BF16),
            pltpu.VMEM(w_up.shape, BF16),
            pltpu.VMEM(w_down.shape, BF16),
        ),
        in_specs=[hbm] * 11,
        out_specs=(vmem,) * 7,
        scratch_shapes=[
            pltpu.VMEM((features, query_count), jnp.int32),
            pltpu.VMEM((own, features), jnp.int32),
            pltpu.VMEM((1, own), jnp.int32),
            pltpu.VMEM(bin_table.shape, BF16),
            pltpu.VMEM(rank_vector.shape, BF16),
            pltpu.VMEM(w_query.shape, BF16),
            pltpu.VMEM(w_key.shape, BF16),
            pltpu.VMEM(w_value.shape, BF16),
            pltpu.SemaphoreType.DMA((11,)),
            pltpu.VMEM((lines, LANES), jnp.int32),
            pltpu.VMEM((count, lines, LANES), jnp.int32),
            pltpu.VMEM((total, width), F32),
            pltpu.VMEM((total, width), BF16),
            pltpu.SemaphoreType.DMA,
            pltpu.SemaphoreType.DMA,
        ],
        compiler_params=pltpu.CompilerParams(
            collective_id=0, has_side_effects=True, vmem_limit_bytes=EMBED_LIMIT
        ),
        name="embed_rows",
    )(
        *(
            pltpu.with_memory_space_constraint(value, pltpu.HBM)
            for value in (
                query_bins.T,
                hist_bins,
                hist_ranks.reshape(1, own),
                bin_table,
                rank_vector,
                w_query,
                w_key,
                w_value,
                w_out,
                w_up,
                w_down,
            )
        )
    )
    groups = query_count // (2 * query_tile)
    return pl.pallas_call(
        functools.partial(layer_kernel, query_tile),
        out_shape=(
            jax.ShapeDtypeStruct((own, width), BF16),
            jax.ShapeDtypeStruct((query_count, width), BF16),
        ),
        in_specs=[vmem] * 7,
        out_specs=(hbm, hbm),
        scratch_shapes=[
            pltpu.VMEM((row_count, width), BF16),
            pltpu.VMEM((AHEAD + 2, hist_tile, query_tile), F32),
            pltpu.VMEM((2 * query_tile + own, w_up.shape[1]), BF16),
            pltpu.SemaphoreType.DMA((2 * groups + 1,)),
        ],
        compiler_params=pltpu.CompilerParams(vmem_limit_bytes=LAYER_LIMIT),
        name="layer_rows",
    )(*held)


def solution(mesh):
    split = P(("ctx", "qry"), None)
    return jax.shard_map(
        functools.partial(local, mesh.shape["ctx"], mesh.shape["qry"]),
        mesh=mesh,
        in_specs=(split, P(("ctx", "qry")), split) + (P(),) * 8,
        out_specs=(split, split),
        check_vma=False,
    )
```

```python
import functools
import math

import jax
import jax.numpy as jnp
from jax import lax
from jax.experimental import pallas as pl
from jax.experimental.pallas import tpu as pltpu
from jax.sharding import PartitionSpec as P

HEADS = 8
LANES = 128
EMBED_LIMIT = 24 << 20
LAYER_LIMIT = 28 << 20
GROUP = 8
UP_TILE = 256
DOWN_TILE = 256
SPLIT = 2
AHEAD = 2
BEHIND = 1
epsilon = 1e-05
GELU = math.sqrt(2.0 / math.pi)
F32 = jnp.float32
BF16 = jnp.bfloat16


def normalize(values):
    centered = values - jnp.mean(values, axis=-1, keepdims=True)
    variance = jnp.mean(centered * centered, axis=-1, keepdims=True)
    return centered * lax.rsqrt(variance + epsilon)


def dot(a, b):
    return jnp.dot(a, b, preferred_element_type=F32)


def dot_rows(a, b):
    return lax.dot_general(a, b, (((1,), (1,)), ((), ())), preferred_element_type=F32)


def iota(shape, dim):
    return lax.broadcasted_iota(jnp.int32, shape, dim)


def one(mask):
    return jnp.where(mask, 1.0, 0.0).astype(BF16)


def embed(named, column_bin, table):
    return dot(one(named == column_bin), table)


def embed_kernel(
    sizes,
    query_bins_hbm,
    hist_bins_hbm,
    hist_ranks_hbm,
    table_hbm,
    rank_vector_hbm,
    w_query_hbm,
    w_key_hbm,
    w_value_hbm,
    w_out_hbm,
    w_up_hbm,
    w_down_hbm,
    rows_out,
    queries_out,
    keys_out,
    values_out,
    w_out,
    w_up,
    w_down,
    query_bins,
    hist_bins,
    hist_ranks,
    table,
    rank_vector,
    w_query,
    w_key,
    w_value,
    fetch_sem,
    mine,
    blocks,
    hist_rows,
    hist_normed,
    send_sem,
    recv_sem,
):
    outer, inner, query_tile, hist_tile, hist_part = sizes
    count = outer * inner
    own, features = hist_bins.shape
    query_count = query_bins.shape[1]
    total = count * own
    fetches = [
        pltpu.make_async_copy(source, target, fetch_sem.at[index])
        for index, (source, target) in enumerate(
            (
                (hist_bins_hbm, hist_bins),
                (hist_ranks_hbm, hist_ranks),
                (query_bins_hbm, query_bins),
                (table_hbm, table),
                (w_query_hbm, w_query),
                (rank_vector_hbm, rank_vector),
                (w_key_hbm, w_key),
                (w_value_hbm, w_value),
                (w_out_hbm, w_out),
                (w_up_hbm, w_up),
                (w_down_hbm, w_down),
            )
        )
    ]
    for fetch in fetches[:8]:
        fetch.start()
    at_outer = lax.axis_index("ctx")
    at_inner = lax.axis_index("qry")
    chips = outer // 2
    chip, core = at_outer // 2, at_outer % 2
    quarter = count // 4
    twin = {"ctx": chip * 2 + 1 - core, "qry": at_inner}
    barrier = pltpu.get_barrier_semaphore()

    def others(side, act):
        def across(turn, carry):
            for place in range(chips):
                act(
                    {
                        "ctx": (chip + chips - 1 - place) % chips * 2 + core,
                        "qry": (at_inner + 2 * inner - 1 - turn) % inner,
                    },
                    turn * chips + place,
                )
            return carry

        half = inner // 2
        if side == 0:
            lax.fori_loop(0, half, across, 0)
        else:
            lax.fori_loop(half, inner - 1, across, 0)
            for place in range(chips - 1):
                act(
                    {"ctx": (chip + chips - 1 - place) % chips * 2 + core, "qry": at_inner},
                    (inner - 1) * chips + place,
                )

    def slot(side, half):
        return (side * 2 + half) * quarter

    def greet(device, index):
        pl.semaphore_signal(
            barrier, inc=1, device_id=device, device_id_type=pl.DeviceIdType.MESH
        )

    others(0, greet)
    others(1, greet)
    greet(twin, 0)

    parts = features // GROUP
    per_row = iota((own, LANES), 1) // GROUP == iota((own, LANES), 0)
    fetches[0].wait()
    fetches[1].wait()
    bins = hist_bins[...].astype(F32).astype(BF16)
    for part in range(parts):
        pick = iota((features, LANES), 1) % GROUP + part * GROUP == iota((features, LANES), 0)
        laid = jnp.sum(jnp.where(per_row, dot(bins, one(pick)), 0.0), axis=0, keepdims=True)
        mine[part : part + 1, :] = laid.astype(jnp.int32)
    mine[parts : parts + 1, :] = jnp.zeros((1, LANES), jnp.int32)
    mine[parts : parts + 1, :own] = hist_ranks[...]
    blocks[slot(1, 0) + quarter - 1] = mine[...]

    def sender(side):
        def send(device, index):
            pltpu.make_async_remote_copy(
                src_ref=mine,
                dst_ref=blocks.at[index + slot(side, 0) - side * quarter],
                send_sem=send_sem.at[side],
                recv_sem=recv_sem.at[side],
                device_id=device,
                device_id_type=pl.DeviceIdType.MESH,
            ).start()

        return send

    pl.semaphore_wait(barrier, count // 2)
    for side in range(2):
        others(side, sender(side))

    def span(side, half):
        size = quarter - 1 if side and not half else quarter
        return blocks.at[pl.ds(slot(side, half), size)]

    def settle(side, half, sem):
        pltpu.make_async_copy(span(side, half), span(side, half), sem).wait()

    def forward(side):
        mirror = blocks.at[pl.ds(slot(side, 0), quarter)]
        return pltpu.make_async_remote_copy(
            src_ref=mirror,
            dst_ref=blocks.at[pl.ds(slot(side, 1), quarter)],
            send_sem=send_sem.at[2 + side],
            recv_sem=recv_sem.at[2 + side],
            device_id=twin,
            device_id_type=pl.DeviceIdType.MESH,
        )

    bin_count = table.shape[0] // features
    wide = (features, table.shape[0])
    spread = one(iota(wide, 1) // bin_count == iota(wide, 0))
    column_bin = (iota((1, table.shape[0]), 1) % bin_count).astype(F32)
    width = table.shape[1]
    head_dim = width // HEADS
    pairs = HEADS // 2
    factor = math.log2(math.e) * head_dim ** (-0.5)

    def project(normed):
        return (dot(normed, w_query[...]) * factor).astype(BF16)

    for fetch in fetches[2:5]:
        fetch.wait()
    for fetch in fetches[8:]:
        fetch.start()

    def query_step(index, carry):
        at = pl.ds(pl.multiple_of(index * query_tile, query_tile), query_tile)
        named = lax.dot_general(
            query_bins[:, at].astype(F32).astype(BF16),
            spread,
            (((0,), (0,)), ((), ())),
            preferred_element_type=F32,
        )
        found = embed(named, column_bin, table[...])
        rows_out[at, :] = found
        queries_out[at, :] = project(normalize(found).astype(BF16))
        return carry

    lax.fori_loop(0, query_count // query_tile, query_step, 0)

    for fetch in fetches[5:8]:
        fetch.wait()
    tall = (parts * LANES, table.shape[0])
    deal = one(
        iota(tall, 1) // bin_count == iota(tall, 0) // LANES * GROUP + iota(tall, 0) % GROUP
    )
    tile_blocks = hist_part // own
    block_shape = (tile_blocks, own, LANES)
    lane = iota(block_shape, 2)
    row = iota(block_shape, 1)
    left = iota((hist_part, LANES), 1) < head_dim
    in_chunk = hist_tile // hist_part

    def hist_step(index, carry):
        chunk = index // in_chunk
        start = pl.multiple_of(index % in_chunk * hist_part, hist_part)
        at = pl.ds(pl.multiple_of(index * hist_part, hist_part), hist_part)
        block = blocks[pl.ds(index * tile_blocks, tile_blocks)].astype(F32)
        laid = [
            jnp.where(lane // GROUP == row, block[:, part : part + 1, :], 0.0)
            .reshape(hist_part, LANES)
            .astype(BF16)
            for part in range(parts)
        ]
        rank = jnp.sum(
            jnp.where(lane == row, block[:, parts : parts + 1, :], 0.0).reshape(
                hist_part, LANES
            ),
            axis=1,
            keepdims=True,
        )
        level = (2.0 * rank + 1.0) / float(total) - 1.0
        found = embed(dot(jnp.concatenate(laid, axis=1), deal), column_bin, table[...])
        found = found + level * rank_vector[...].astype(F32).reshape(1, -1)
        hist_rows[at, :] = found
        normed = normalize(found).astype(BF16)
        hist_normed[at, :] = normed
        keys = dot(normed, w_key[...])
        values = dot(normed, w_value[...]).astype(BF16).T
        for pair in range(pairs):
            key = keys[:, pair * LANES : (pair + 1) * LANES]
            for half, mine_only in ((0, left), (1, jnp.logical_not(left))):
                keys_out[chunk, pair, pl.ds(start + half * hist_tile, hist_part), :] = jnp.where(
                    mine_only, key, 0.0
                ).astype(BF16)
        for head in range(HEADS):
            values_out[chunk, head, :head_dim, pl.ds(start, hist_part)] = values[
                head * head_dim : (head + 1) * head_dim, :
            ]
            values_out[chunk, head, head_dim:, pl.ds(start, hist_part)] = jnp.ones(
                (values_out.shape[2] - head_dim, hist_part), BF16
            )
        return carry

    for side in range(2):
        settle(side, 0, recv_sem.at[side])
        forward(side).start()
    for side in range(2):
        settle(side, 1, recv_sem.at[2 + side])
        steps = total // 2 // hist_part
        lax.fori_loop(side * steps, (side + 1) * steps, hist_step, 0)
    start = (slot(1, 0) + quarter - 1) * own
    rows_out[query_count:, :] = hist_rows[start : start + own, :]
    queries_out[query_count:, :] = project(hist_normed[start : start + own, :])
    for side in range(2):
        settle(side, 0, send_sem.at[side])
        settle(side, 1, send_sem.at[2 + side])
    for fetch in fetches[8:]:
        fetch.wait()


def layer_kernel(
    tile,
    rows,
    queries,
    keys,
    values,
    w_out,
    w_up,
    w_down,
    hist_out,
    query_out,
    results,
    scores,
    hidden,
    store_sem,
):
    own, width = hist_out.shape
    query_count = query_out.shape[0]
    head_dim = width // HEADS
    chunks = keys.shape[0]
    length = keys.shape[2] // 2
    part = length // SPLIT
    slots = scores.shape[0]

    def project(at, attended):
        after = rows[at, :] + dot(jnp.concatenate(attended, axis=0).T, w_out[...])
        rows[at, :] = after
        queries[at, :] = normalize(after).astype(BF16)

    def asked(at, head):
        pair = head // 2
        return queries[at, pair * LANES : (pair + 1) * LANES]

    def quotient(summed):
        return (summed[:head_dim] / summed[head_dim : head_dim + 1]).astype(BF16)

    def attend_whole(tiles):
        units = [(at, head) for at in tiles for head in range(HEADS)]
        peaks, weights, attended = {}, {}, {}

        def score(unit, piece):
            at, head = units[unit]
            start = head % 2 * length + piece * part
            found = dot_rows(keys[0, head // 2, start : start + part], asked(at, head))
            scores[unit % slots, piece * part : (piece + 1) * part, : found.shape[1]] = found
            peak = jnp.max(found, axis=0, keepdims=True)
            peaks[unit] = jnp.maximum(peaks[unit], peak) if piece else peak

        def weigh(unit, piece):
            peak = peaks[unit]
            span = slice(piece * part, (piece + 1) * part)
            found = scores[unit % slots, span, : peak.shape[1]]
            weights[unit, piece] = jnp.exp2(found - peak).astype(BF16)

        def gather(unit):
            at, head = units[unit]
            pieces = [weights.pop((unit, piece)) for piece in range(SPLIT)]
            summed = dot(values[0, head], jnp.concatenate(pieces, axis=0))
            attended[head] = quotient(summed)
            if head == HEADS - 1:
                project(at, [attended[index] for index in range(HEADS)])

        for step in range(-AHEAD, len(units) + BEHIND):
            for piece in range(SPLIT):
                if step + AHEAD < len(units):
                    score(step + AHEAD, piece)
                if 0 <= step < len(units):
                    weigh(step, piece)
                if piece == SPLIT - 1 and step >= BEHIND:
                    gather(step - BEHIND)
                yield

    def attend_chunks(tiles):
        for at in tiles:
            attended = []
            for head in range(HEADS):
                half = head % 2 * length
                query = asked(at, head)
                lanes = query.shape[0]

                def absorb(chunk, carry):
                    peak, summed = carry
                    found = dot_rows(keys[chunk, head // 2, half : half + length], query)
                    new = jnp.maximum(peak, jnp.max(found, axis=0, keepdims=True))
                    weights = jnp.exp2(found - new).astype(BF16)
                    summed = summed * jnp.exp2(peak - new) + dot(values[chunk, head], weights)
                    return new, summed

                empty = (
                    jnp.full((1, lanes), -jnp.inf, F32),
                    jnp.zeros((values.shape[2], lanes), F32),
                )
                attended.append(quotient(lax.fori_loop(0, chunks, absorb, empty)[1]))
                yield
            project(at, attended)

    stores = []

    def store(source, target):
        copy = pltpu.make_async_copy(source, target, store_sem.at[len(stores)])
        copy.start()
        stores.append(copy)

    def feed(start, middle, stop):
        for first in range(0, w_up.shape[1], UP_TILE):
            span = slice(first, first + UP_TILE)
            value = dot(queries[start:stop, :], w_up[:, span]).astype(BF16)
            bend = jnp.tanh(value * (value * value * (0.044715 * GELU) + GELU))
            hidden[: stop - start, span] = value + value * bend
            yield 2 * (stop - start)
        for low, high in ((start, middle), (middle, stop)):
            for first in range(0, width, DOWN_TILE):
                span = slice(first, first + DOWN_TILE)
                fed = dot(hidden[low - start : high - start, :], w_down[:, span])
                results[low:high, span] = (rows[low:high, span] + 0.5 * fed).astype(BF16)
                yield 8 * (high - low)
            queried = min(high, query_count)
            store(results.at[low:queried], query_out.at[low:queried])
            if high > queried:
                store(results.at[queried:high], hist_out)

    group = 2 * tile
    pending, cost = iter(()), 0
    for start in range(0, query_count, group):
        stop = min(start + group, query_count)
        tiles = [slice(first, first + tile) for first in range(start, stop, tile)]
        if stop == query_count:
            tiles.insert(1, slice(query_count, query_count + own))
            stop += own
        attend = attend_whole if chunks == 1 else attend_chunks
        if chunks == 1:
            steps = (len(tiles) * HEADS + AHEAD + BEHIND) * SPLIT
        else:
            steps = len(tiles) * HEADS
        done = 0
        for index, _ in enumerate(attend(tiles)):
            while done < cost * (index + 1) / steps:
                done += next(pending, cost)
        for _ in pending:
            pass
        pending = feed(start, start + tile, stop)
        cost = 2 * (stop - start) * (w_up.shape[1] // UP_TILE) * 2
    for _ in pending:
        pass
    for copy in stores:
        copy.wait()


def local(
    outer,
    inner,
    hist_bins,
    hist_ranks,
    query_bins,
    bin_table,
    rank_vector,
    w_query,
    w_key,
    w_value,
    w_out,
    w_up,
    w_down,
):
    own, features = hist_bins.shape
    query_count = query_bins.shape[0]
    width = bin_table.shape[1]
    count = outer * inner
    total = own * count
    row_count = own + query_count
    hist_tile = math.gcd(total, 512)
    hist_part = math.gcd(total // 2, 256)
    query_tile = math.gcd(query_count, 256)
    chunks = total // hist_tile
    pairs = HEADS // 2
    tall = width // HEADS + 16
    lines = features // GROUP + 1
    hbm = pl.BlockSpec(memory_space=pltpu.HBM)
    vmem = pl.BlockSpec(memory_space=pltpu.VMEM)
    held = pl.pallas_call(
        functools.partial(embed_kernel, (outer, inner, query_tile, hist_tile, hist_part)),
        out_shape=(
            pltpu.VMEM((row_count, width), F32),
            pltpu.VMEM((row_count, width), BF16),
            pltpu.VMEM((chunks, pairs, 2 * hist_tile, LANES), BF16),
            pltpu.VMEM((chunks, HEADS, tall, hist_tile), BF16),
            pltpu.VMEM(w_out.shape, BF16),
            pltpu.VMEM(w_up.shape, BF16),
            pltpu.VMEM(w_down.shape, BF16),
        ),
        in_specs=[hbm] * 11,
        out_specs=(vmem,) * 7,
        scratch_shapes=[
            pltpu.VMEM((features, query_count), jnp.int32),
            pltpu.VMEM((own, features), jnp.int32),
            pltpu.VMEM((1, own), jnp.int32),
            pltpu.VMEM(bin_table.shape, BF16),
            pltpu.VMEM(rank_vector.shape, BF16),
            pltpu.VMEM(w_query.shape, BF16),
            pltpu.VMEM(w_key.shape, BF16),
            pltpu.VMEM(w_value.shape, BF16),
            pltpu.SemaphoreType.DMA((11,)),
            pltpu.VMEM((lines, LANES), jnp.int32),
            pltpu.VMEM((count, lines, LANES), jnp.int32),
            pltpu.VMEM((total, width), F32),
            pltpu.VMEM((total, width), BF16),
            pltpu.SemaphoreType.DMA((4,)),
            pltpu.SemaphoreType.DMA((4,)),
        ],
        compiler_params=pltpu.CompilerParams(
            collective_id=0, has_side_effects=True, vmem_limit_bytes=EMBED_LIMIT
        ),
        name="embed_rows",
    )(
        *(
            pltpu.with_memory_space_constraint(value, pltpu.HBM)
            for value in (
                query_bins.T,
                hist_bins,
                hist_ranks.reshape(1, own),
                bin_table,
                rank_vector,
                w_query,
                w_key,
                w_value,
                w_out,
                w_up,
                w_down,
            )
        )
    )
    groups = query_count // (2 * query_tile)
    return pl.pallas_call(
        functools.partial(layer_kernel, query_tile),
        out_shape=(
            jax.ShapeDtypeStruct((own, width), BF16),
            jax.ShapeDtypeStruct((query_count, width), BF16),
        ),
        in_specs=[vmem] * 7,
        out_specs=(hbm, hbm),
        scratch_shapes=[
            pltpu.VMEM((row_count, width), BF16),
            pltpu.VMEM((AHEAD + 2, hist_tile, query_tile), F32),
            pltpu.VMEM((2 * query_tile + own, w_up.shape[1]), BF16),
            pltpu.SemaphoreType.DMA((2 * groups + 1,)),
        ],
        compiler_params=pltpu.CompilerParams(vmem_limit_bytes=LAYER_LIMIT),
        name="layer_rows",
    )(*held)


def solution(mesh):
    split = P(("ctx", "qry"), None)
    return jax.shard_map(
        functools.partial(local, mesh.shape["ctx"], mesh.shape["qry"]),
        mesh=mesh,
        in_specs=(split, P(("ctx", "qry")), split) + (P(),) * 8,
        out_specs=(split, split),
        check_vma=False,
    )
```

```python
import functools
import math

import jax
import jax.numpy as jnp
from jax import lax
from jax.experimental import pallas as pl
from jax.experimental.pallas import tpu as pltpu
from jax.sharding import PartitionSpec as P

HEADS = 8
LANES = 128
EMBED_LIMIT = 8 << 20
LAYER_LIMIT = 40 << 20
GROUP = 8
UP_TILE = 256
DOWN_TILE = 256
SPLIT = 2
AHEAD = 2
BEHIND = 1
epsilon = 1e-05
GELU = math.sqrt(2.0 / math.pi)
F32 = jnp.float32
BF16 = jnp.bfloat16


def normalize(values):
    centered = values - jnp.mean(values, axis=-1, keepdims=True)
    variance = jnp.mean(centered * centered, axis=-1, keepdims=True)
    return centered * lax.rsqrt(variance + epsilon)


def dot(a, b):
    return jnp.dot(a, b, preferred_element_type=F32)


def dot_rows(a, b):
    return lax.dot_general(a, b, (((1,), (1,)), ((), ())), preferred_element_type=F32)


def iota(shape, dim):
    return lax.broadcasted_iota(jnp.int32, shape, dim)


def one(mask):
    return jnp.where(mask, 1.0, 0.0).astype(BF16)


def embed(named, column_bin, table):
    return dot(one(named == column_bin), table)


def ask(normed, w_query):
    factor = math.log2(math.e) * (w_query.shape[1] // HEADS) ** (-0.5)
    return (dot(normed, w_query) * factor).astype(BF16)


def embed_kernel(
    sizes,
    query_bins_hbm,
    hist_bins_hbm,
    hist_ranks_hbm,
    table_hbm,
    rank_vector_hbm,
    w_query_hbm,
    w_key_hbm,
    w_value_hbm,
    w_out_hbm,
    w_up_hbm,
    w_down_hbm,
    rows_out,
    queries_out,
    blocks_out,
    table,
    rank_vector,
    w_query,
    w_key,
    w_value,
    w_out,
    w_up,
    w_down,
    query_bins,
    hist_bins,
    hist_ranks,
    fetch_sem,
    mine,
    blocks,
    send_sem,
    recv_sem,
):
    outer, inner, query_tile = sizes
    count = outer * inner
    own, features = hist_bins.shape
    query_count = query_bins.shape[1]
    fetches = [
        pltpu.make_async_copy(source, target, fetch_sem.at[index])
        for index, (source, target) in enumerate(
            (
                (hist_bins_hbm, hist_bins),
                (hist_ranks_hbm, hist_ranks),
                (query_bins_hbm, query_bins),
                (table_hbm, table),
                (w_query_hbm, w_query),
                (rank_vector_hbm, rank_vector),
                (w_key_hbm, w_key),
                (w_value_hbm, w_value),
                (w_out_hbm, w_out),
                (w_up_hbm, w_up),
                (w_down_hbm, w_down),
            )
        )
    ]
    for fetch in fetches[:2]:
        fetch.start()
    at_outer = lax.axis_index("ctx")
    at_inner = lax.axis_index("qry")
    barrier = pltpu.get_barrier_semaphore()

    def others(act):
        def across(step, carry):
            for shift in reversed(range(outer)):
                act(
                    {
                        "ctx": (at_outer + shift) % outer,
                        "qry": (at_inner + inner - step) % inner,
                    },
                    step * outer + shift,
                )
            return carry

        lax.fori_loop(1, inner, across, 0)
        for shift in reversed(range(1, outer)):
            act({"ctx": (at_outer + shift) % outer, "qry": at_inner}, shift)

    def greet(device, slot):
        pl.semaphore_signal(
            barrier, inc=1, device_id=device, device_id_type=pl.DeviceIdType.MESH
        )

    others(greet)
    for fetch in fetches[2:8]:
        fetch.start()

    parts = features // GROUP
    per_row = iota((own, LANES), 1) // GROUP == iota((own, LANES), 0)
    fetches[0].wait()
    fetches[1].wait()
    bins = hist_bins[...].astype(F32).astype(BF16)
    for part in range(parts):
        pick = iota((features, LANES), 1) % GROUP + part * GROUP == iota((features, LANES), 0)
        laid = jnp.sum(jnp.where(per_row, dot(bins, one(pick)), 0.0), axis=0, keepdims=True)
        mine[part : part + 1, :] = laid.astype(jnp.int32)
    mine[parts : parts + 1, :] = jnp.zeros((1, LANES), jnp.int32)
    mine[parts : parts + 1, :own] = hist_ranks[...]
    blocks[0] = mine[...]

    def send(device, slot):
        pltpu.make_async_remote_copy(
            src_ref=mine,
            dst_ref=blocks.at[slot],
            send_sem=send_sem,
            recv_sem=recv_sem,
            device_id=device,
            device_id_type=pl.DeviceIdType.MESH,
        ).start()

    pl.semaphore_wait(barrier, count - 1)
    others(send)

    bin_count = table.shape[0] // features
    wide = (features, table.shape[0])
    spread = one(iota(wide, 1) // bin_count == iota(wide, 0))
    column_bin = (iota((1, table.shape[0]), 1) % bin_count).astype(F32)

    for fetch in fetches[2:5]:
        fetch.wait()
    for fetch in fetches[8:]:
        fetch.start()

    def query_step(index, carry):
        at = pl.ds(pl.multiple_of(index * query_tile, query_tile), query_tile)
        named = lax.dot_general(
            query_bins[:, at].astype(F32).astype(BF16),
            spread,
            (((0,), (0,)), ((), ())),
            preferred_element_type=F32,
        )
        found = embed(named, column_bin, table[...])
        rows_out[at, :] = found
        queries_out[at, :] = ask(normalize(found).astype(BF16), w_query[...])
        return carry

    lax.fori_loop(0, query_count // query_tile, query_step, 0)

    rest = blocks.at[pl.ds(1, count - 1)]
    pltpu.make_async_copy(rest, rest, recv_sem).wait()
    blocks_out[...] = blocks[...]
    for fetch in fetches[5:]:
        fetch.wait()
    pltpu.make_async_copy(rest, rest, send_sem).wait()


def layer_kernel(
    sizes,
    rows,
    queries,
    blocks,
    table,
    rank_vector,
    w_query,
    w_key,
    w_value,
    w_out,
    w_up,
    w_down,
    hist_out,
    query_out,
    keys,
    values,
    own_rows,
    own_queries,
    after,
    normed_after,
    results,
    scores,
    hidden,
    store_sem,
):
    tile, features = sizes
    own, width = hist_out.shape
    query_count = query_out.shape[0]
    head_dim = width // HEADS
    pairs = HEADS // 2
    chunks = keys.shape[0]
    length = keys.shape[2] // 2
    part = length // SPLIT
    slots = scores.shape[0]
    own_at = slice(query_count, query_count + own)

    bin_count = table.shape[0] // features
    per_tile = LANES // bin_count
    parts = features // GROUP
    part_blocks = part // own
    block_shape = (part_blocks, own, LANES)
    lane = iota((part, LANES), 1)
    row = iota((part, LANES), 0) % own
    bin_here = lane % bin_count
    left = lane < head_dim

    def spread_out(block, line):
        return jnp.broadcast_to(block[:, line : line + 1, :], block_shape).reshape(part, LANES)

    def find(block):
        one_hot = []
        for line in range(parts):
            laid = spread_out(block, line)
            for first in range(0, GROUP, per_tile):
                source = row * GROUP + first + lane // bin_count
                named = jnp.take_along_axis(laid, source, axis=1, mode="promise_in_bounds")
                one_hot.append(one(named == bin_here))
        ranks = jnp.where(lane == row, spread_out(block, parts).astype(F32), 0.0)
        rank = jnp.sum(ranks, axis=1, keepdims=True)
        level = (2.0 * rank + 1.0) / float(chunks * length) - 1.0
        found = dot(jnp.concatenate(one_hot, axis=1), table[...])
        return found + level * rank_vector[...].astype(F32).reshape(1, -1)

    def fill(chunk, keep):
        first = chunk * (length // own)
        found = [
            find(blocks[pl.ds(first + piece * part_blocks, part_blocks)])
            for piece in range(SPLIT)
        ]
        for piece in range(SPLIT):
            normed = normalize(found[piece]).astype(BF16)
            if keep and piece == 0:
                own_rows[...] = found[0][:own]
                own_queries[...] = ask(normed[:own], w_query[...])
            key = dot(normed, w_key[...])
            low, high = piece * part, (piece + 1) * part
            for pair in range(pairs):
                pair_key = key[:, pair * LANES : (pair + 1) * LANES]
                keys[chunk, pair, low:high, :] = jnp.where(left, pair_key, 0.0).astype(BF16)
                keys[chunk, pair, length + low : length + high, :] = jnp.where(
                    left, 0.0, pair_key
                ).astype(BF16)
            value = dot(normed, w_value[...]).astype(BF16).T
            for head in range(HEADS):
                values[chunk, head, :head_dim, low:high] = value[
                    head * head_dim : (head + 1) * head_dim, :
                ]
        values[chunk, :, head_dim:, :] = jnp.ones(
            (HEADS, values.shape[2] - head_dim, length), BF16
        )

    fill(0, True)
    if chunks > 1:

        def fill_next(chunk, carry):
            fill(chunk, False)
            return carry

        lax.fori_loop(1, chunks, fill_next, 0)

    def project(at, attended):
        before = own_rows[...] if at == own_at else rows[at, :]
        summed = before + dot(jnp.concatenate(attended, axis=0).T, w_out[...])
        after[at, :] = summed
        normed_after[at, :] = normalize(summed).astype(BF16)

    def asked(at, head):
        span = slice(head // 2 * LANES, (head // 2 + 1) * LANES)
        return own_queries[:, span] if at == own_at else queries[at, span]

    def quotient(summed):
        return (summed[:head_dim] / summed[head_dim : head_dim + 1]).astype(BF16)

    def attend_whole(tiles):
        units = [(at, head) for at in tiles for head in range(HEADS)]
        peaks, weights, attended = {}, {}, {}

        def score(unit, piece):
            at, head = units[unit]
            start = head % 2 * length + piece * part
            found = dot_rows(keys[0, head // 2, start : start + part], asked(at, head))
            scores[unit % slots, piece * part : (piece + 1) * part, : found.shape[1]] = found
            peak = jnp.max(found, axis=0, keepdims=True)
            peaks[unit] = jnp.maximum(peaks[unit], peak) if piece else peak

        def weigh(unit, piece):
            peak = peaks[unit]
            span = slice(piece * part, (piece + 1) * part)
            found = scores[unit % slots, span, : peak.shape[1]]
            weights[unit, piece] = jnp.exp2(found - peak).astype(BF16)

        def gather(unit):
            at, head = units[unit]
            pieces = [weights.pop((unit, piece)) for piece in range(SPLIT)]
            summed = dot(values[0, head], jnp.concatenate(pieces, axis=0))
            attended[head] = quotient(summed)
            if head == HEADS - 1:
                project(at, [attended[index] for index in range(HEADS)])

        for step in range(-AHEAD, len(units) + BEHIND):
            for piece in range(SPLIT):
                if step + AHEAD < len(units):
                    score(step + AHEAD, piece)
                if 0 <= step < len(units):
                    weigh(step, piece)
                if piece == SPLIT - 1 and step >= BEHIND:
                    gather(step - BEHIND)
                yield

    def attend_chunks(tiles):
        for at in tiles:
            attended = []
            for head in range(HEADS):
                half = head % 2 * length
                query = asked(at, head)
                lanes = query.shape[0]

                def absorb(chunk, carry):
                    peak, summed = carry
                    found = dot_rows(keys[chunk, head // 2, half : half + length], query)
                    new = jnp.maximum(peak, jnp.max(found, axis=0, keepdims=True))
                    weights = jnp.exp2(found - new).astype(BF16)
                    summed = summed * jnp.exp2(peak - new) + dot(values[chunk, head], weights)
                    return new, summed

                empty = (
                    jnp.full((1, lanes), -jnp.inf, F32),
                    jnp.zeros((values.shape[2], lanes), F32),
                )
                attended.append(quotient(lax.fori_loop(0, chunks, absorb, empty)[1]))
                yield
            project(at, attended)

    stores = []

    def store(source, target):
        copy = pltpu.make_async_copy(source, target, store_sem.at[len(stores)])
        copy.start()
        stores.append(copy)

    def feed(start, middle, stop):
        for first in range(0, w_up.shape[1], UP_TILE):
            span = slice(first, first + UP_TILE)
            value = dot(normed_after[start:stop, :], w_up[:, span]).astype(BF16)
            bend = jnp.tanh(value * (value * value * (0.044715 * GELU) + GELU))
            hidden[: stop - start, span] = value + value * bend
            yield 2 * (stop - start)
        for low, high in ((start, middle), (middle, stop)):
            for first in range(0, width, DOWN_TILE):
                span = slice(first, first + DOWN_TILE)
                fed = dot(hidden[low - start : high - start, :], w_down[:, span])
                results[low:high, span] = (after[low:high, span] + 0.5 * fed).astype(BF16)
                yield 8 * (high - low)
            queried = min(high, query_count)
            store(results.at[low:queried], query_out.at[low:queried])
            if high > queried:
                store(results.at[queried:high], hist_out)

    group = 2 * tile
    pending, cost = iter(()), 0
    for start in range(0, query_count, group):
        stop = min(start + group, query_count)
        tiles = [slice(first, first + tile) for first in range(start, stop, tile)]
        if stop == query_count:
            tiles.insert(1, own_at)
            stop += own
        attend = attend_whole if chunks == 1 else attend_chunks
        if chunks == 1:
            steps = (len(tiles) * HEADS + AHEAD + BEHIND) * SPLIT
        else:
            steps = len(tiles) * HEADS
        done = 0
        for index, _ in enumerate(attend(tiles)):
            while done < cost * (index + 1) / steps:
                done += next(pending, cost)
        for _ in pending:
            pass
        pending = feed(start, start + tile, stop)
        cost = 2 * (stop - start) * (w_up.shape[1] // UP_TILE) * 2
    for _ in pending:
        pass
    for copy in stores:
        copy.wait()


def local(
    outer,
    inner,
    hist_bins,
    hist_ranks,
    query_bins,
    bin_table,
    rank_vector,
    w_query,
    w_key,
    w_value,
    w_out,
    w_up,
    w_down,
):
    own, features = hist_bins.shape
    query_count = query_bins.shape[0]
    width = bin_table.shape[1]
    count = outer * inner
    total = own * count
    row_count = own + query_count
    hist_tile = math.gcd(total, 512)
    query_tile = math.gcd(query_count, 256)
    chunks = total // hist_tile
    pairs = HEADS // 2
    tall = width // HEADS + 16
    lines = features // GROUP + 1
    hbm = pl.BlockSpec(memory_space=pltpu.HBM)
    vmem = pl.BlockSpec(memory_space=pltpu.VMEM)
    held = pl.pallas_call(
        functools.partial(embed_kernel, (outer, inner, query_tile)),
        out_shape=(
            pltpu.VMEM((row_count, width), F32),
            pltpu.VMEM((row_count, width), BF16),
            pltpu.VMEM((count, lines, LANES), jnp.int32),
            pltpu.VMEM(bin_table.shape, BF16),
            pltpu.VMEM(rank_vector.shape, BF16),
            pltpu.VMEM(w_query.shape, BF16),
            pltpu.VMEM(w_key.shape, BF16),
            pltpu.VMEM(w_value.shape, BF16),
            pltpu.VMEM(w_out.shape, BF16),
            pltpu.VMEM(w_up.shape, BF16),
            pltpu.VMEM(w_down.shape, BF16),
        ),
        in_specs=[hbm] * 11,
        out_specs=(vmem,) * 11,
        scratch_shapes=[
            pltpu.VMEM((features, query_count), jnp.int32),
            pltpu.VMEM((own, features), jnp.int32),
            pltpu.VMEM((1, own), jnp.int32),
            pltpu.SemaphoreType.DMA((11,)),
            pltpu.VMEM((lines, LANES), jnp.int32),
            pltpu.VMEM((count, lines, LANES), jnp.int32),
            pltpu.SemaphoreType.DMA,
            pltpu.SemaphoreType.DMA,
        ],
        compiler_params=pltpu.CompilerParams(
            collective_id=0, has_side_effects=True, vmem_limit_bytes=EMBED_LIMIT
        ),
        name="embed_rows",
    )(
        *(
            pltpu.with_memory_space_constraint(value, pltpu.HBM)
            for value in (
                query_bins.T,
                hist_bins,
                hist_ranks.reshape(1, own),
                bin_table,
                rank_vector,
                w_query,
                w_key,
                w_value,
                w_out,
                w_up,
                w_down,
            )
        )
    )
    groups = query_count // (2 * query_tile)
    return pl.pallas_call(
        functools.partial(layer_kernel, (query_tile, features)),
        out_shape=(
            jax.ShapeDtypeStruct((own, width), BF16),
            jax.ShapeDtypeStruct((query_count, width), BF16),
        ),
        in_specs=[vmem] * 11,
        out_specs=(hbm, hbm),
        scratch_shapes=[
            pltpu.VMEM((chunks, pairs, 2 * hist_tile, LANES), BF16),
            pltpu.VMEM((chunks, HEADS, tall, hist_tile), BF16),
            pltpu.VMEM((own, width), F32),
            pltpu.VMEM((own, width), BF16),
            pltpu.VMEM((row_count, width), F32),
            pltpu.VMEM((row_count, width), BF16),
            pltpu.VMEM((row_count, width), BF16),
            pltpu.VMEM((AHEAD + 2, hist_tile, query_tile), F32),
            pltpu.VMEM((2 * query_tile + own, w_up.shape[1]), BF16),
            pltpu.SemaphoreType.DMA((2 * groups + 1,)),
        ],
        compiler_params=pltpu.CompilerParams(vmem_limit_bytes=LAYER_LIMIT),
        name="layer_rows",
    )(*held)


def solution(mesh):
    split = P(("ctx", "qry"), None)
    return jax.shard_map(
        functools.partial(local, mesh.shape["ctx"], mesh.shape["qry"]),
        mesh=mesh,
        in_specs=(split, P(("ctx", "qry")), split) + (P(),) * 8,
        out_specs=(split, split),
        check_vma=False,
    )
```

```python
import functools
import math

import jax
import jax.numpy as jnp
from jax import lax
from jax.experimental import pallas as pl
from jax.experimental.pallas import tpu as pltpu
from jax.sharding import PartitionSpec as P

HEADS = 8
LANES = 128
SLACK = 0.9
EMBED_LIMIT = 8 << 20
LAYER_LIMIT = 40 << 20
GROUP = 8
UP_TILE = 256
DOWN_TILE = 256
SPLIT = 2
AHEAD = 2
BEHIND = 1
epsilon = 1e-05
GELU = math.sqrt(2.0 / math.pi)
F32 = jnp.float32
BF16 = jnp.bfloat16


def normalize(values):
    centered = values - jnp.mean(values, axis=-1, keepdims=True)
    variance = jnp.mean(centered * centered, axis=-1, keepdims=True)
    return centered * lax.rsqrt(variance + epsilon)


def dot(a, b):
    return jnp.dot(a, b, preferred_element_type=F32)


def dot_rows(a, b):
    return lax.dot_general(a, b, (((1,), (1,)), ((), ())), preferred_element_type=F32)


def iota(shape, dim):
    return lax.broadcasted_iota(jnp.int32, shape, dim)


def one(mask):
    return jnp.where(mask, 1.0, 0.0).astype(BF16)


def embed(named, column_bin, table):
    return dot(one(named == column_bin), table)


def ask(normed, w_query):
    factor = math.log2(math.e) * (w_query.shape[1] // HEADS) ** (-0.5)
    return (dot(normed, w_query) * factor).astype(BF16)


def embed_kernel(
    sizes,
    query_bins_hbm,
    hist_bins_hbm,
    hist_ranks_hbm,
    table_hbm,
    rank_vector_hbm,
    w_query_hbm,
    w_key_hbm,
    w_value_hbm,
    w_out_hbm,
    w_up_hbm,
    w_down_hbm,
    rows_out,
    queries_out,
    blocks_out,
    table,
    rank_vector,
    w_query,
    w_key,
    w_value,
    w_out,
    w_up,
    w_down,
    query_bins,
    hist_bins,
    hist_ranks,
    fetch_sem,
    mine,
    blocks,
    send_sem,
    recv_sem,
):
    outer, inner, query_tile = sizes
    count = outer * inner
    own, features = hist_bins.shape
    query_count = query_bins.shape[1]
    fetches = [
        pltpu.make_async_copy(source, target, fetch_sem.at[index])
        for index, (source, target) in enumerate(
            (
                (hist_bins_hbm, hist_bins),
                (hist_ranks_hbm, hist_ranks),
                (query_bins_hbm, query_bins),
                (table_hbm, table),
                (w_query_hbm, w_query),
                (rank_vector_hbm, rank_vector),
                (w_key_hbm, w_key),
                (w_value_hbm, w_value),
                (w_out_hbm, w_out),
                (w_up_hbm, w_up),
                (w_down_hbm, w_down),
            )
        )
    ]
    for fetch in fetches[:2]:
        fetch.start()
    at_outer = lax.axis_index("ctx")
    at_inner = lax.axis_index("qry")
    barrier = pltpu.get_barrier_semaphore()

    def others(act):
        def across(step, carry):
            for shift in reversed(range(outer)):
                act(
                    {
                        "ctx": (at_outer + shift) % outer,
                        "qry": (at_inner + inner - step) % inner,
                    },
                    step * outer + shift,
                )
            return carry

        lax.fori_loop(1, inner, across, 0)
        for shift in reversed(range(1, outer)):
            act({"ctx": (at_outer + shift) % outer, "qry": at_inner}, shift)

    def greet(device, slot):
        pl.semaphore_signal(
            barrier, inc=1, device_id=device, device_id_type=pl.DeviceIdType.MESH
        )

    others(greet)
    for fetch in fetches[2:8]:
        fetch.start()

    parts = features // GROUP
    per_row = iota((own, LANES), 1) // GROUP == iota((own, LANES), 0)
    fetches[0].wait()
    fetches[1].wait()
    bins = hist_bins[...].astype(F32).astype(BF16)
    for part in range(parts):
        pick = iota((features, LANES), 1) % GROUP + part * GROUP == iota((features, LANES), 0)
        laid = jnp.sum(jnp.where(per_row, dot(bins, one(pick)), 0.0), axis=0, keepdims=True)
        mine[part : part + 1, :] = laid.astype(jnp.int32)
    mine[parts : parts + 1, :] = jnp.zeros((1, LANES), jnp.int32)
    mine[parts : parts + 1, :own] = hist_ranks[...]
    blocks[0] = mine[...]

    def send(device, slot):
        pltpu.make_async_remote_copy(
            src_ref=mine,
            dst_ref=blocks.at[slot],
            send_sem=send_sem,
            recv_sem=recv_sem,
            device_id=device,
            device_id_type=pl.DeviceIdType.MESH,
        ).start()

    pl.semaphore_wait(barrier, count - 1)
    others(send)

    bin_count = table.shape[0] // features
    wide = (features, table.shape[0])
    spread = one(iota(wide, 1) // bin_count == iota(wide, 0))
    column_bin = (iota((1, table.shape[0]), 1) % bin_count).astype(F32)

    for fetch in fetches[2:5]:
        fetch.wait()
    for fetch in fetches[8:]:
        fetch.start()

    def query_step(index, carry):
        at = pl.ds(pl.multiple_of(index * query_tile, query_tile), query_tile)
        named = lax.dot_general(
            query_bins[:, at].astype(F32).astype(BF16),
            spread,
            (((0,), (0,)), ((), ())),
            preferred_element_type=F32,
        )
        found = embed(named, column_bin, table[...])
        rows_out[at, :] = found
        queries_out[at, :] = ask(normalize(found).astype(BF16), w_query[...])
        return carry

    lax.fori_loop(0, query_count // query_tile, query_step, 0)

    rest = blocks.at[pl.ds(1, count - 1)]
    pltpu.make_async_copy(rest, rest, recv_sem).wait()
    blocks_out[...] = blocks[...]
    for fetch in fetches[5:]:
        fetch.wait()
    pltpu.make_async_copy(rest, rest, send_sem).wait()


def layer_kernel(
    sizes,
    rows,
    queries,
    blocks,
    table,
    rank_vector,
    w_query,
    w_key,
    w_value,
    w_out,
    w_up,
    w_down,
    hist_out,
    query_out,
    keys,
    values,
    own_rows,
    own_queries,
    after,
    normed_after,
    results,
    scores,
    hidden,
    store_sem,
):
    tile, features = sizes
    own, width = hist_out.shape
    query_count = query_out.shape[0]
    head_dim = width // HEADS
    pairs = HEADS // 2
    chunks = keys.shape[0]
    length = keys.shape[2] // 2
    part = length // SPLIT
    slots = scores.shape[0]
    own_at = slice(query_count, query_count + own)

    bin_count = table.shape[0] // features
    per_tile = LANES // bin_count
    parts = features // GROUP
    part_blocks = part // own
    block_shape = (part_blocks, own, LANES)
    lane = iota((part, LANES), 1)
    row = iota((part, LANES), 0) % own
    bin_here = lane % bin_count
    left = lane < head_dim
    tall = (parts * LANES, table.shape[0])
    deal = one(
        iota(tall, 1) // bin_count == iota(tall, 0) // LANES * GROUP + iota(tall, 0) % GROUP
    )
    column_bin = (iota((1, table.shape[0]), 1) % bin_count).astype(F32)

    def spread_out(block, line):
        return jnp.broadcast_to(block[:, line : line + 1, :], block_shape).reshape(part, LANES)

    def find(block):
        laid = [
            jnp.where(lane // GROUP == row, spread_out(block, line).astype(F32), 0.0).astype(BF16)
            for line in range(parts)
        ]
        named = dot(jnp.concatenate(laid, axis=1), deal)
        one_hot = [one(named == column_bin)]
        ranks = jnp.where(lane == row, spread_out(block, parts).astype(F32), 0.0)
        rank = jnp.sum(ranks, axis=1, keepdims=True)
        level = (2.0 * rank + 1.0) / float(chunks * length) - 1.0
        found = dot(jnp.concatenate(one_hot, axis=1), table[...])
        return found + level * rank_vector[...].astype(F32).reshape(1, -1)

    def fill(chunk, keep):
        first = chunk * (length // own)
        found = [
            find(blocks[pl.ds(first + piece * part_blocks, part_blocks)])
            for piece in range(SPLIT)
        ]
        for piece in range(SPLIT):
            normed = normalize(found[piece]).astype(BF16)
            if keep and piece == 0:
                own_rows[...] = found[0][:own]
                own_queries[...] = ask(normed[:own], w_query[...])
            key = dot(normed, w_key[...])
            low, high = piece * part, (piece + 1) * part
            for pair in range(pairs):
                pair_key = key[:, pair * LANES : (pair + 1) * LANES]
                keys[chunk, pair, low:high, :] = jnp.where(left, pair_key, 0.0).astype(BF16)
                keys[chunk, pair, length + low : length + high, :] = jnp.where(
                    left, 0.0, pair_key
                ).astype(BF16)
            value = dot(normed, w_value[...]).astype(BF16).T
            for head in range(HEADS):
                values[chunk, head, :head_dim, low:high] = value[
                    head * head_dim : (head + 1) * head_dim, :
                ]
        values[chunk, :, head_dim:, :] = jnp.ones(
            (HEADS, values.shape[2] - head_dim, length), BF16
        )

    fill(0, True)
    if chunks > 1:

        def fill_next(chunk, carry):
            fill(chunk, False)
            return carry

        lax.fori_loop(1, chunks, fill_next, 0)

    def project(at, attended):
        before = own_rows[...] if at == own_at else rows[at, :]
        summed = before + dot(jnp.concatenate(attended, axis=0).T, w_out[...])
        after[at, :] = summed
        normed_after[at, :] = normalize(summed).astype(BF16)

    def asked(at, head):
        span = slice(head // 2 * LANES, (head // 2 + 1) * LANES)
        return own_queries[:, span] if at == own_at else queries[at, span]

    def quotient(summed):
        return (summed[:head_dim] / summed[head_dim : head_dim + 1]).astype(BF16)

    def attend_whole(tiles):
        units = [(at, head) for at in tiles for head in range(HEADS)]
        peaks, weights, attended = {}, {}, {}

        def score(unit, piece):
            at, head = units[unit]
            start = head % 2 * length + piece * part
            found = dot_rows(keys[0, head // 2, start : start + part], asked(at, head))
            scores[unit % slots, piece * part : (piece + 1) * part, : found.shape[1]] = found
            peak = jnp.max(found, axis=0, keepdims=True)
            peaks[unit] = jnp.maximum(peaks[unit], peak) if piece else peak

        def weigh(unit, piece):
            peak = peaks[unit]
            span = slice(piece * part, (piece + 1) * part)
            found = scores[unit % slots, span, : peak.shape[1]]
            weights[unit, piece] = jnp.exp2(found - peak).astype(BF16)

        def gather(unit):
            at, head = units[unit]
            pieces = [weights.pop((unit, piece)) for piece in range(SPLIT)]
            summed = dot(values[0, head], jnp.concatenate(pieces, axis=0))
            attended[head] = quotient(summed)
            if head == HEADS - 1:
                project(at, [attended[index] for index in range(HEADS)])

        for step in range(-AHEAD, len(units) + BEHIND):
            for piece in range(SPLIT):
                if step + AHEAD < len(units):
                    score(step + AHEAD, piece)
                if 0 <= step < len(units):
                    weigh(step, piece)
                if piece == SPLIT - 1 and step >= BEHIND:
                    gather(step - BEHIND)
                yield

    def attend_chunks(tiles):
        for at in tiles:
            attended = []
            for head in range(HEADS):
                half = head % 2 * length
                query = asked(at, head)
                lanes = query.shape[0]

                def absorb(chunk, carry):
                    peak, summed = carry
                    found = dot_rows(keys[chunk, head // 2, half : half + length], query)
                    new = jnp.maximum(peak, jnp.max(found, axis=0, keepdims=True))
                    weights = jnp.exp2(found - new).astype(BF16)
                    summed = summed * jnp.exp2(peak - new) + dot(values[chunk, head], weights)
                    return new, summed

                empty = (
                    jnp.full((1, lanes), -jnp.inf, F32),
                    jnp.zeros((values.shape[2], lanes), F32),
                )
                attended.append(quotient(lax.fori_loop(0, chunks, absorb, empty)[1]))
                yield
            project(at, attended)

    stores = []

    def store(source, target):
        copy = pltpu.make_async_copy(source, target, store_sem.at[len(stores)])
        copy.start()
        stores.append(copy)

    def feed(start, middle, stop):
        for first in range(0, w_up.shape[1], UP_TILE):
            span = slice(first, first + UP_TILE)
            value = dot(normed_after[start:stop, :], w_up[:, span]).astype(BF16)
            bend = jnp.tanh(value * (value * value * (0.044715 * GELU) + GELU))
            hidden[: stop - start, span] = value + value * bend
            yield 2 * (stop - start)
        for low, high in ((start, middle), (middle, stop)):
            for first in range(0, width, DOWN_TILE):
                span = slice(first, first + DOWN_TILE)
                fed = dot(hidden[low - start : high - start, :], w_down[:, span])
                results[low:high, span] = (after[low:high, span] + 0.5 * fed).astype(BF16)
                yield 8 * (high - low)
            queried = min(high, query_count)
            store(results.at[low:queried], query_out.at[low:queried])
            if high > queried:
                store(results.at[queried:high], hist_out)

    tiles = [slice(first, first + tile) for first in range(0, query_count, tile)]
    groups = [tiles[first : first + 2] for first in range(0, len(tiles), 2)]
    groups[-1] = groups[-1][:1] + [own_at] + groups[-1][1:]
    order = [at for members in groups for at in members]
    if chunks == 1:
        walk, pace, lead = attend_whole(order), SPLIT, (AHEAD + BEHIND) * SPLIT
    else:
        walk, pace, lead = attend_chunks(order), 1, 1
    steps = len(order) * HEADS * pace + lead
    done_at, count = [], 0
    for members in groups:
        count += len(members) * HEADS * pace
        done_at.append(count + lead)
    pending, cost, done, begun, at_group = iter(()), 0, 0, 0, 0
    for index in range(steps + 1):
        next(walk, None)
        if index + 1 >= done_at[at_group]:
            for _ in pending:
                pass
            start = groups[at_group][0].start
            stop = max(at.stop for at in groups[at_group])
            pending = feed(start, start + tile, stop)
            cost, done, begun = 4 * (stop - start) * (w_up.shape[1] // UP_TILE), 0, index
            at_group += 1
            if at_group == len(groups):
                break
        span = done_at[at_group] - 1 - begun
        while done < cost * (index - begun) / (span * SLACK):
            done += next(pending, cost)
    for _ in walk:
        pass
    for _ in pending:
        pass
    for copy in stores:
        copy.wait()


def local(
    outer,
    inner,
    hist_bins,
    hist_ranks,
    query_bins,
    bin_table,
    rank_vector,
    w_query,
    w_key,
    w_value,
    w_out,
    w_up,
    w_down,
):
    own, features = hist_bins.shape
    query_count = query_bins.shape[0]
    width = bin_table.shape[1]
    count = outer * inner
    total = own * count
    row_count = own + query_count
    hist_tile = math.gcd(total, 512)
    query_tile = math.gcd(query_count, 256)
    chunks = total // hist_tile
    pairs = HEADS // 2
    tall = width // HEADS + 16
    lines = features // GROUP + 1
    hbm = pl.BlockSpec(memory_space=pltpu.HBM)
    vmem = pl.BlockSpec(memory_space=pltpu.VMEM)
    held = pl.pallas_call(
        functools.partial(embed_kernel, (outer, inner, query_tile)),
        out_shape=(
            pltpu.VMEM((row_count, width), F32),
            pltpu.VMEM((row_count, width), BF16),
            pltpu.VMEM((count, lines, LANES), jnp.int32),
            pltpu.VMEM(bin_table.shape, BF16),
            pltpu.VMEM(rank_vector.shape, BF16),
            pltpu.VMEM(w_query.shape, BF16),
            pltpu.VMEM(w_key.shape, BF16),
            pltpu.VMEM(w_value.shape, BF16),
            pltpu.VMEM(w_out.shape, BF16),
            pltpu.VMEM(w_up.shape, BF16),
            pltpu.VMEM(w_down.shape, BF16),
        ),
        in_specs=[hbm] * 11,
        out_specs=(vmem,) * 11,
        scratch_shapes=[
            pltpu.VMEM((features, query_count), jnp.int32),
            pltpu.VMEM((own, features), jnp.int32),
            pltpu.VMEM((1, own), jnp.int32),
            pltpu.SemaphoreType.DMA((11,)),
            pltpu.VMEM((lines, LANES), jnp.int32),
            pltpu.VMEM((count, lines, LANES), jnp.int32),
            pltpu.SemaphoreType.DMA,
            pltpu.SemaphoreType.DMA,
        ],
        compiler_params=pltpu.CompilerParams(
            collective_id=0, has_side_effects=True, vmem_limit_bytes=EMBED_LIMIT
        ),
        name="embed_rows",
    )(
        *(
            pltpu.with_memory_space_constraint(value, pltpu.HBM)
            for value in (
                query_bins.T,
                hist_bins,
                hist_ranks.reshape(1, own),
                bin_table,
                rank_vector,
                w_query,
                w_key,
                w_value,
                w_out,
                w_up,
                w_down,
            )
        )
    )
    groups = query_count // (2 * query_tile)
    return pl.pallas_call(
        functools.partial(layer_kernel, (query_tile, features)),
        out_shape=(
            jax.ShapeDtypeStruct((own, width), BF16),
            jax.ShapeDtypeStruct((query_count, width), BF16),
        ),
        in_specs=[vmem] * 11,
        out_specs=(hbm, hbm),
        scratch_shapes=[
            pltpu.VMEM((chunks, pairs, 2 * hist_tile, LANES), BF16),
            pltpu.VMEM((chunks, HEADS, tall, hist_tile), BF16),
            pltpu.VMEM((own, width), F32),
            pltpu.VMEM((own, width), BF16),
            pltpu.VMEM((row_count, width), F32),
            pltpu.VMEM((row_count, width), BF16),
            pltpu.VMEM((row_count, width), BF16),
            pltpu.VMEM((AHEAD + 2, hist_tile, query_tile), F32),
            pltpu.VMEM((2 * query_tile + own, w_up.shape[1]), BF16),
            pltpu.SemaphoreType.DMA((2 * groups + 1,)),
        ],
        compiler_params=pltpu.CompilerParams(vmem_limit_bytes=LAYER_LIMIT),
        name="layer_rows",
    )(*held)


def solution(mesh):
    split = P(("ctx", "qry"), None)
    return jax.shard_map(
        functools.partial(local, mesh.shape["ctx"], mesh.shape["qry"]),
        mesh=mesh,
        in_specs=(split, P(("ctx", "qry")), split) + (P(),) * 8,
        out_specs=(split, split),
        check_vma=False,
    )
```

```python
import functools
import math

import jax
import jax.numpy as jnp
from jax import lax
from jax.experimental import pallas as pl
from jax.experimental.pallas import tpu as pltpu
from jax.sharding import PartitionSpec as P

HEADS = 8
LANES = 128
SLACK = 0.9
EMBED_LIMIT = 8 << 20
LAYER_LIMIT = 40 << 20
GROUP = 8
UP_TILE = 256
DOWN_TILE = 256
SPLIT = 2
AHEAD = 2
BEHIND = 1
epsilon = 1e-05
GELU = math.sqrt(2.0 / math.pi)
F32 = jnp.float32
BF16 = jnp.bfloat16


def normalize(values):
    centered = values - jnp.mean(values, axis=-1, keepdims=True)
    variance = jnp.mean(centered * centered, axis=-1, keepdims=True)
    return centered * lax.rsqrt(variance + epsilon)


def dot(a, b):
    return jnp.dot(a, b, preferred_element_type=F32)


def dot_rows(a, b):
    return lax.dot_general(a, b, (((1,), (1,)), ((), ())), preferred_element_type=F32)


def iota(shape, dim):
    return lax.broadcasted_iota(jnp.int32, shape, dim)


def one(mask):
    return jnp.where(mask, 1.0, 0.0).astype(BF16)


def embed(named, column_bin, table):
    return dot(one(named == column_bin), table)


def ask(normed, w_query):
    factor = math.log2(math.e) * (w_query.shape[1] // HEADS) ** (-0.5)
    return (dot(normed, w_query) * factor).astype(BF16)


def embed_kernel(
    sizes,
    query_bins_hbm,
    hist_bins_hbm,
    hist_ranks_hbm,
    table_hbm,
    rank_vector_hbm,
    w_query_hbm,
    w_key_hbm,
    w_value_hbm,
    w_out_hbm,
    w_up_hbm,
    w_down_hbm,
    rows_out,
    queries_out,
    blocks_out,
    table,
    rank_vector,
    w_query,
    w_key,
    w_value,
    w_out,
    w_up,
    w_down,
    query_bins,
    hist_bins,
    hist_ranks,
    fetch_sem,
    mine,
    blocks,
    send_sem,
    recv_sem,
):
    outer, inner, query_tile = sizes
    count = outer * inner
    own, features = hist_bins.shape
    query_count = query_bins.shape[1]
    fetches = [
        pltpu.make_async_copy(source, target, fetch_sem.at[index])
        for index, (source, target) in enumerate(
            (
                (hist_bins_hbm, hist_bins),
                (hist_ranks_hbm, hist_ranks),
                (query_bins_hbm, query_bins),
                (table_hbm, table),
                (w_query_hbm, w_query),
                (rank_vector_hbm, rank_vector),
                (w_key_hbm, w_key),
                (w_value_hbm, w_value),
                (w_out_hbm, w_out),
                (w_up_hbm, w_up),
                (w_down_hbm, w_down),
            )
        )
    ]
    for fetch in fetches[:2]:
        fetch.start()
    at_outer = lax.axis_index("ctx")
    at_inner = lax.axis_index("qry")
    barrier = pltpu.get_barrier_semaphore()

    def others(act):
        def across(step, carry):
            for shift in reversed(range(outer)):
                act(
                    {
                        "ctx": (at_outer + shift) % outer,
                        "qry": (at_inner + inner - step) % inner,
                    },
                    step * outer + shift,
                )
            return carry

        lax.fori_loop(1, inner, across, 0, unroll=inner <= 4)
        for shift in reversed(range(1, outer)):
            act({"ctx": (at_outer + shift) % outer, "qry": at_inner}, shift)

    def greet(device, slot):
        pl.semaphore_signal(
            barrier, inc=1, device_id=device, device_id_type=pl.DeviceIdType.MESH
        )

    others(greet)
    for fetch in fetches[2:8]:
        fetch.start()

    parts = features // GROUP
    per_row = iota((own, LANES), 1) // GROUP == iota((own, LANES), 0)
    fetches[0].wait()
    fetches[1].wait()
    bins = hist_bins[...].astype(F32).astype(BF16)
    for part in range(parts):
        pick = iota((features, LANES), 1) % GROUP + part * GROUP == iota((features, LANES), 0)
        laid = jnp.sum(jnp.where(per_row, dot(bins, one(pick)), 0.0), axis=0, keepdims=True)
        mine[part : part + 1, :] = laid.astype(jnp.int32)
    mine[parts : parts + 1, :] = jnp.zeros((1, LANES), jnp.int32)
    mine[parts : parts + 1, :own] = hist_ranks[...]
    blocks[0] = mine[...]

    def send(device, slot):
        pltpu.make_async_remote_copy(
            src_ref=mine,
            dst_ref=blocks.at[slot],
            send_sem=send_sem,
            recv_sem=recv_sem,
            device_id=device,
            device_id_type=pl.DeviceIdType.MESH,
        ).start()

    pl.semaphore_wait(barrier, count - 1)
    others(send)

    bin_count = table.shape[0] // features
    wide = (features, table.shape[0])
    spread = one(iota(wide, 1) // bin_count == iota(wide, 0))
    column_bin = (iota((1, table.shape[0]), 1) % bin_count).astype(F32)

    for fetch in fetches[2:5]:
        fetch.wait()
    for fetch in fetches[8:]:
        fetch.start()

    def query_step(index, carry):
        at = pl.ds(pl.multiple_of(index * query_tile, query_tile), query_tile)
        named = lax.dot_general(
            query_bins[:, at].astype(F32).astype(BF16),
            spread,
            (((0,), (0,)), ((), ())),
            preferred_element_type=F32,
        )
        found = embed(named, column_bin, table[...])
        rows_out[at, :] = found
        queries_out[at, :] = ask(normalize(found).astype(BF16), w_query[...])
        return carry

    lax.fori_loop(0, query_count // query_tile, query_step, 0)

    rest = blocks.at[pl.ds(1, count - 1)]
    pltpu.make_async_copy(rest, rest, recv_sem).wait()
    blocks_out[...] = blocks[...]
    for fetch in fetches[5:]:
        fetch.wait()
    pltpu.make_async_copy(rest, rest, send_sem).wait()


def layer_kernel(
    sizes,
    rows,
    queries,
    blocks,
    table,
    rank_vector,
    w_query,
    w_key,
    w_value,
    w_out,
    w_up,
    w_down,
    hist_out,
    query_out,
    keys,
    values,
    own_rows,
    own_queries,
    after,
    normed_after,
    results,
    scores,
    hidden,
    store_sem,
):
    tile, features = sizes
    own, width = hist_out.shape
    query_count = query_out.shape[0]
    head_dim = width // HEADS
    pairs = HEADS // 2
    chunks = keys.shape[0]
    length = keys.shape[2] // 2
    part = length // SPLIT
    slots = scores.shape[0]
    own_at = slice(query_count, query_count + own)

    bin_count = table.shape[0] // features
    per_tile = LANES // bin_count
    parts = features // GROUP
    part_blocks = part // own
    block_shape = (part_blocks, own, LANES)
    lane = iota((part, LANES), 1)
    row = iota((part, LANES), 0) % own
    bin_here = lane % bin_count
    left = lane < head_dim
    tall = (parts * LANES, table.shape[0])
    deal = one(
        iota(tall, 1) // bin_count == iota(tall, 0) // LANES * GROUP + iota(tall, 0) % GROUP
    )
    column_bin = (iota((1, table.shape[0]), 1) % bin_count).astype(F32)

    def spread_out(block, line):
        return jnp.broadcast_to(block[:, line : line + 1, :], block_shape).reshape(part, LANES)

    def find(block):
        laid = [
            jnp.where(lane // GROUP == row, spread_out(block, line).astype(F32), 0.0).astype(BF16)
            for line in range(parts)
        ]
        named = dot(jnp.concatenate(laid, axis=1), deal)
        one_hot = [one(named == column_bin)]
        ranks = jnp.where(lane == row, spread_out(block, parts).astype(F32), 0.0)
        rank = jnp.sum(ranks, axis=1, keepdims=True)
        level = (2.0 * rank + 1.0) / float(chunks * length) - 1.0
        found = dot(jnp.concatenate(one_hot, axis=1), table[...])
        return found + level * rank_vector[...].astype(F32).reshape(1, -1)

    def fill(chunk, keep):
        first = chunk * (length // own)
        found = [
            find(blocks[pl.ds(first + piece * part_blocks, part_blocks)])
            for piece in range(SPLIT)
        ]
        for piece in range(SPLIT):
            normed = normalize(found[piece]).astype(BF16)
            if keep and piece == 0:
                own_rows[...] = found[0][:own]
                own_queries[...] = ask(normed[:own], w_query[...])
            key = dot(normed, w_key[...])
            low, high = piece * part, (piece + 1) * part
            for pair in range(pairs):
                pair_key = key[:, pair * LANES : (pair + 1) * LANES]
                keys[chunk, pair, low:high, :] = jnp.where(left, pair_key, 0.0).astype(BF16)
                keys[chunk, pair, length + low : length + high, :] = jnp.where(
                    left, 0.0, pair_key
                ).astype(BF16)
            value = dot(normed, w_value[...]).astype(BF16).T
            for head in range(HEADS):
                values[chunk, head, :head_dim, low:high] = value[
                    head * head_dim : (head + 1) * head_dim, :
                ]
        values[chunk, :, head_dim:, :] = jnp.ones(
            (HEADS, values.shape[2] - head_dim, length), BF16
        )

    fill(0, True)
    if chunks > 1:

        def fill_next(chunk, carry):
            fill(chunk, False)
            return carry

        lax.fori_loop(1, chunks, fill_next, 0)

    def project(at, attended):
        before = own_rows[...] if at == own_at else rows[at, :]
        summed = before + dot(jnp.concatenate(attended, axis=0).T, w_out[...])
        after[at, :] = summed
        normed_after[at, :] = normalize(summed).astype(BF16)

    def asked(at, head):
        span = slice(head // 2 * LANES, (head // 2 + 1) * LANES)
        return own_queries[:, span] if at == own_at else queries[at, span]

    def quotient(summed):
        return (summed[:head_dim] / summed[head_dim : head_dim + 1]).astype(BF16)

    def attend_whole(tiles):
        units = [(at, head) for at in tiles for head in range(HEADS)]
        peaks, weights, attended = {}, {}, {}

        def score(unit, piece):
            at, head = units[unit]
            start = head % 2 * length + piece * part
            found = dot_rows(keys[0, head // 2, start : start + part], asked(at, head))
            scores[unit % slots, piece * part : (piece + 1) * part, : found.shape[1]] = found
            peak = jnp.max(found, axis=0, keepdims=True)
            peaks[unit] = jnp.maximum(peaks[unit], peak) if piece else peak

        def weigh(unit, piece):
            peak = peaks[unit]
            span = slice(piece * part, (piece + 1) * part)
            found = scores[unit % slots, span, : peak.shape[1]]
            weights[unit, piece] = jnp.exp2(found - peak).astype(BF16)

        def gather(unit):
            at, head = units[unit]
            pieces = [weights.pop((unit, piece)) for piece in range(SPLIT)]
            summed = dot(values[0, head], jnp.concatenate(pieces, axis=0))
            attended[head] = quotient(summed)
            if head == HEADS - 1:
                project(at, [attended[index] for index in range(HEADS)])

        for step in range(-AHEAD, len(units) + BEHIND):
            for piece in range(SPLIT):
                if step + AHEAD < len(units):
                    score(step + AHEAD, piece)
                if 0 <= step < len(units):
                    weigh(step, piece)
                if piece == SPLIT - 1 and step >= BEHIND:
                    gather(step - BEHIND)
                yield

    def attend_chunks(tiles):
        for at in tiles:
            attended = []
            for head in range(HEADS):
                half = head % 2 * length
                query = asked(at, head)
                lanes = query.shape[0]

                def absorb(chunk, carry):
                    peak, summed = carry
                    found = dot_rows(keys[chunk, head // 2, half : half + length], query)
                    new = jnp.maximum(peak, jnp.max(found, axis=0, keepdims=True))
                    weights = jnp.exp2(found - new).astype(BF16)
                    summed = summed * jnp.exp2(peak - new) + dot(values[chunk, head], weights)
                    return new, summed

                empty = (
                    jnp.full((1, lanes), -jnp.inf, F32),
                    jnp.zeros((values.shape[2], lanes), F32),
                )
                attended.append(quotient(lax.fori_loop(0, chunks, absorb, empty)[1]))
                yield
            project(at, attended)

    stores = []

    def store(source, target):
        copy = pltpu.make_async_copy(source, target, store_sem.at[len(stores)])
        copy.start()
        stores.append(copy)

    def feed(start, middle, stop):
        for first in range(0, w_up.shape[1], UP_TILE):
            span = slice(first, first + UP_TILE)
            value = dot(normed_after[start:stop, :], w_up[:, span]).astype(BF16)
            bend = jnp.tanh(value * (value * value * (0.044715 * GELU) + GELU))
            hidden[: stop - start, span] = value + value * bend
            yield 2 * (stop - start)
        for low, high in ((start, middle), (middle, stop)):
            for first in range(0, width, DOWN_TILE):
                span = slice(first, first + DOWN_TILE)
                fed = dot(hidden[low - start : high - start, :], w_down[:, span])
                results[low:high, span] = (after[low:high, span] + 0.5 * fed).astype(BF16)
                yield 8 * (high - low)
            queried = min(high, query_count)
            store(results.at[low:queried], query_out.at[low:queried])
            if high > queried:
                store(results.at[queried:high], hist_out)

    tiles = [slice(first, first + tile) for first in range(0, query_count, tile)]
    groups = [tiles[first : first + 2] for first in range(0, len(tiles), 2)]
    groups[-1] = groups[-1][:1] + [own_at] + groups[-1][1:]
    order = [at for members in groups for at in members]
    if chunks == 1:
        walk, pace, lead = attend_whole(order), SPLIT, (AHEAD + BEHIND) * SPLIT
    else:
        walk, pace, lead = attend_chunks(order), 1, 1
    steps = len(order) * HEADS * pace + lead
    done_at, count = [], 0
    for members in groups:
        count += len(members) * HEADS * pace
        done_at.append(count + lead)
    pending, cost, done, begun, at_group = iter(()), 0, 0, 0, 0
    for index in range(steps + 1):
        next(walk, None)
        if index + 1 >= done_at[at_group]:
            for _ in pending:
                pass
            start = groups[at_group][0].start
            stop = max(at.stop for at in groups[at_group])
            pending = feed(start, start + tile, stop)
            cost, done, begun = 4 * (stop - start) * (w_up.shape[1] // UP_TILE), 0, index
            at_group += 1
            if at_group == len(groups):
                break
        span = done_at[at_group] - 1 - begun
        while done < cost * (index - begun) / (span * SLACK):
            done += next(pending, cost)
    for _ in walk:
        pass
    for _ in pending:
        pass
    for copy in stores:
        copy.wait()


def local(
    outer,
    inner,
    hist_bins,
    hist_ranks,
    query_bins,
    bin_table,
    rank_vector,
    w_query,
    w_key,
    w_value,
    w_out,
    w_up,
    w_down,
):
    own, features = hist_bins.shape
    query_count = query_bins.shape[0]
    width = bin_table.shape[1]
    count = outer * inner
    total = own * count
    row_count = own + query_count
    hist_tile = math.gcd(total, 512)
    query_tile = math.gcd(query_count, 256)
    chunks = total // hist_tile
    pairs = HEADS // 2
    tall = width // HEADS + 16
    lines = features // GROUP + 1
    hbm = pl.BlockSpec(memory_space=pltpu.HBM)
    vmem = pl.BlockSpec(memory_space=pltpu.VMEM)
    held = pl.pallas_call(
        functools.partial(embed_kernel, (outer, inner, query_tile)),
        out_shape=(
            pltpu.VMEM((row_count, width), F32),
            pltpu.VMEM((row_count, width), BF16),
            pltpu.VMEM((count, lines, LANES), jnp.int32),
            pltpu.VMEM(bin_table.shape, BF16),
            pltpu.VMEM(rank_vector.shape, BF16),
            pltpu.VMEM(w_query.shape, BF16),
            pltpu.VMEM(w_key.shape, BF16),
            pltpu.VMEM(w_value.shape, BF16),
            pltpu.VMEM(w_out.shape, BF16),
            pltpu.VMEM(w_up.shape, BF16),
            pltpu.VMEM(w_down.shape, BF16),
        ),
        in_specs=[hbm] * 11,
        out_specs=(vmem,) * 11,
        scratch_shapes=[
            pltpu.VMEM((features, query_count), jnp.int32),
            pltpu.VMEM((own, features), jnp.int32),
            pltpu.VMEM((1, own), jnp.int32),
            pltpu.SemaphoreType.DMA((11,)),
            pltpu.VMEM((lines, LANES), jnp.int32),
            pltpu.VMEM((count, lines, LANES), jnp.int32),
            pltpu.SemaphoreType.DMA,
            pltpu.SemaphoreType.DMA,
        ],
        compiler_params=pltpu.CompilerParams(
            collective_id=0, has_side_effects=True, vmem_limit_bytes=EMBED_LIMIT
        ),
        name="embed_rows",
    )(
        *(
            pltpu.with_memory_space_constraint(value, pltpu.HBM)
            for value in (
                query_bins.T,
                hist_bins,
                hist_ranks.reshape(1, own),
                bin_table,
                rank_vector,
                w_query,
                w_key,
                w_value,
                w_out,
                w_up,
                w_down,
            )
        )
    )
    groups = query_count // (2 * query_tile)
    return pl.pallas_call(
        functools.partial(layer_kernel, (query_tile, features)),
        out_shape=(
            jax.ShapeDtypeStruct((own, width), BF16),
            jax.ShapeDtypeStruct((query_count, width), BF16),
        ),
        in_specs=[vmem] * 11,
        out_specs=(hbm, hbm),
        scratch_shapes=[
            pltpu.VMEM((chunks, pairs, 2 * hist_tile, LANES), BF16),
            pltpu.VMEM((chunks, HEADS, tall, hist_tile), BF16),
            pltpu.VMEM((own, width), F32),
            pltpu.VMEM((own, width), BF16),
            pltpu.VMEM((row_count, width), F32),
            pltpu.VMEM((row_count, width), BF16),
            pltpu.VMEM((row_count, width), BF16),
            pltpu.VMEM((AHEAD + 2, hist_tile, query_tile), F32),
            pltpu.VMEM((2 * query_tile + own, w_up.shape[1]), BF16),
            pltpu.SemaphoreType.DMA((2 * groups + 1,)),
        ],
        compiler_params=pltpu.CompilerParams(vmem_limit_bytes=LAYER_LIMIT),
        name="layer_rows",
    )(*held)


def solution(mesh):
    split = P(("ctx", "qry"), None)
    return jax.shard_map(
        functools.partial(local, mesh.shape["ctx"], mesh.shape["qry"]),
        mesh=mesh,
        in_specs=(split, P(("ctx", "qry")), split) + (P(),) * 8,
        out_specs=(split, split),
        check_vma=False,
    )
```
